512 devices in a mesh: lat: 16 (over x_lo, y, core), lon: 32 (over x_hi, z).
Axes of the slice: x: 4 (x_hi: 2, x_lo: 2; x = x_hi * 2 + x_lo), y: 4, z: 16, core: 2. Of those that a mesh axis runs over, the one named last changes fastest.
Arguments:
- field: float32 [256, 16, 4096], P(None, 'lat', 'lon'), may hold values from -6 to 6
- cotangent: float32 [256, 16, 4096], P(None, 'lat', 'lon'), may hold values from -6 to 6
- conv_weight: float32 [3, 3, 256, 256], replicated, may hold values from -0.125 to 0.125
- spectral_filter: float32 [2, 256, 4096], P(None, None, 'lon'), may hold values from -6 to 6
Outputs:
- output: float32 [256, 16, 4096], P(None, 'lat', 'lon')
- input_grad: float32 [256, 16, 4096], P(None, 'lat', 'lon')
- filter_grad: float32 [2, 256, 4096], P(None, None, 'lon')
The draws below stay inside these ranges and needn't reach their ends.
All inputs are finite; a program needn't handle non-finite values.
Results may differ from the reference program's by a relative error of at most 0.00014.
Values sent between devices are 32-bit elements; how exact they have to be, the bound alone decides.
A program may use at most 64 MiB of HBM per device.

```python
from functools import partial
import jax
import jax.numpy as jnp
from jax import lax

C = 256
LON_DEV = 128
NLAT = 16
NLON = 4096
N_LON = 32


def shard_levels(own_key, extent, shards, low, largest):
    loudness, own = 1.0, jax.random.fold_in(own_key, 6)
    for position, parts in shards:
        draws = jnp.exp(jax.random.uniform(jax.random.fold_in(own, position), (parts,), jnp.float32, low / len(shards), largest / len(shards)))
        loudness = loudness * jnp.repeat(draws, extent[position] // parts).reshape([-1 if axis == position else 1 for axis in range(len(extent))])
    return loudness


def bell_draw(key, dims, width, reach, split=(), kind=jnp.bfloat16):
    result = width * jax.random.normal(key, dims, jnp.float32)
    if split:
        result = result * shard_levels(key, dims, split, -0.22, 0.18)
    return jnp.clip(result, -reach, reach).astype(kind)


def setup_inputs(seed: int = 0) -> dict:
    splits = jax.random.split(jax.random.key(seed), 5)
    return {
        "field": bell_draw(splits[0], (C, NLAT, NLON), 1.0, 6.0, ((1, 16), (2, 32)), jnp.float32),
        "cotangent": bell_draw(splits[1], (C, NLAT, NLON), 1.0, 6.0, ((1, 16), (2, 32)), jnp.float32),
        "conv_weight": bell_draw(splits[2], (3, 3, C, C), (9 * C) ** -0.5, 0.125, (), jnp.float32),
        "spectral_filter": bell_draw(splits[3], (2, C, NLON), 1.0, 6.0, ((2, 32),), jnp.float32),
    }


precise = lax.Precision.HIGHEST

def pad_field(field):
    padded = jnp.pad(field, ((0, 0), (1, 1), (0, 0)))
    return jnp.concatenate([padded[:, :, -1:], padded, padded[:, :, :1]], axis=2)

def apply_taps(padded, taps, lat_rows, columns):
    total = jnp.zeros((taps.shape[2], lat_rows, columns), jnp.float32)
    for tap_row in range(3):
        for tap_col in range(3):
            window = padded[:, tap_row:tap_row + lat_rows, tap_col:tap_col + columns]
            total = total + jnp.einsum('oi,iab->oab', taps[tap_row, tap_col], window, precision=precise)
    return total

def natural_order(spectral_filter):
    places = jnp.arange(NLON, dtype=jnp.int32)
    residue = places % N_LON
    width_bits = N_LON.bit_length() - 1
    flipped = jnp.zeros((NLON,), jnp.int32)
    for bit_pos in range(width_bits):
        flipped = flipped + residue // 2 ** bit_pos % 2 * 2 ** (width_bits - 1 - bit_pos)
    column = (LON_DEV * flipped + places // N_LON).astype(jnp.int32)
    return (spectral_filter[0][:, column], spectral_filter[1][:, column])

def layer(conv_weight, field, spectral_filter):
    mixed = apply_taps(pad_field(field), conv_weight, NLAT, NLON)
    gain_real, gain_imag = natural_order(spectral_filter)
    gain = (gain_real + 1j * gain_imag)[:, None, :]
    spectrum = jnp.fft.fft(mixed, axis=-1)
    shaped = jnp.real(jnp.fft.ifft(gain * spectrum, axis=-1))
    return field + shaped

def reference(field, cotangent, conv_weight, spectral_filter):
    output, pullback = jax.vjp(partial(layer, conv_weight), field, spectral_filter)
    input_grad, filter_grad = pullback(cotangent)
    return (output, input_grad, filter_grad)
```

```python
import functools
import math

import jax
import jax.numpy as jnp
import ml_dtypes
import numpy as np
from jax import lax
from jax.experimental import pallas as pl
from jax.experimental.pallas import tpu as pltpu
from jax.sharding import PartitionSpec as P

MESH = pl.DeviceIdType.MESH
f32, bf16 = jnp.float32, jnp.bfloat16


def split(value):
    high = value.astype(bf16)
    return high, (value - high.astype(f32)).astype(bf16)


def matmul(lhs, rhs, dims):
    return lax.dot_general(lhs, rhs, (dims, ((), ())), preferred_element_type=f32)


def turn(value, angle):
    re, im = value
    c, s = math.cos(angle), math.sin(angle)
    return re * c - im * s, im * c + re * s


def conj(value):
    return value[0], None if value[1] is None else -value[1]


def plus(a, b):
    if a[1] is None or b[1] is None:
        return a[0] + b[0], a[1] if b[1] is None else b[1]
    return a[0] + b[0], a[1] + b[1]


def minus(a, b):
    if a[1] is None or b[1] is None:
        return a[0] - b[0], a[1] if b[1] is None else -b[1]
    return a[0] - b[0], a[1] - b[1]


def real_forward(xs):
    n = len(xs)
    if n == 1:
        return [(xs[0], None)]
    if n == 2:
        return [(xs[0] + xs[1], None), (xs[0] - xs[1], None)]
    even, odd = real_forward(xs[0::2]), real_forward(xs[1::2])
    out = [None] * (n // 2 + 1)
    for r in range(n // 4 + 1):
        e, o = even[r], odd[r]
        if r == 0:
            out[0], out[n // 2] = (e[0] + o[0], None), (e[0] - o[0], None)
        elif r == n // 4:
            out[r] = (e[0], -o[0])
        else:
            o = turn(o, -2 * math.pi * r / n)
            out[r], out[n // 2 - r] = plus(e, o), conj(minus(e, o))
    return out


def real_inverse(spec):
    n = 2 * (len(spec) - 1)
    if n == 2:
        a, b = spec[0][0], spec[1][0]
        return [a + b, a - b]
    even, odd = [None] * (n // 4 + 1), [None] * (n // 4 + 1)
    for r in range(n // 4 + 1):
        a, b = spec[r], spec[n // 2 - r]
        if r == 0:
            even[0], odd[0] = (a[0] + b[0], None), (a[0] - b[0], None)
        elif r == n // 4:
            even[r], odd[r] = (2.0 * a[0], None), (-2.0 * a[1], None)
        else:
            b = conj(b)
            even[r], odd[r] = plus(a, b), turn(minus(a, b), 2 * math.pi * r / n)
    out = [None] * n
    out[0::2], out[1::2] = real_inverse(even), real_inverse(odd)
    return out


def flipped_bits(place, extent):
    width = extent.bit_length() - 1
    return sum((place >> bit & 1) << (width - 1 - bit) for bit in range(width))


def tables(lats, lons, columns):
    groups = lons // lats
    residues = [flipped_bits(slot % groups * lats + slot // groups, lons) for slot in range(lons)]
    m = np.arange(columns)
    inner = 2 * np.pi * (np.outer(m, m) % columns) / columns
    c, s = np.cos(inner), np.sin(inner)
    forward = np.block([[c, -s], [s, c]])
    inverse = np.block([[c, s], [-s, c]]) / (columns * lons)
    mats = []
    for mat in (forward, inverse):
        high = mat.astype(np.float32).astype(ml_dtypes.bfloat16)
        mats += [high, (mat - high.astype(np.float64)).astype(ml_dtypes.bfloat16)]
    outer = 2 * np.pi * np.outer(residues, m) / (columns * lons)
    twiddle = np.stack([np.cos(outer), np.sin(outer)]).astype(np.float32)
    return residues, np.stack(mats), twiddle


def layer_kernel(
    lats, lons, residues,
    field, cot, weight, gain, mats, twiddle,
    out, igrad, fgrad,
    wbuf, wrow_hi, wrow_lo, wcol_hi, wcol_lo, xe, be, windows,
    mixed, cot_line, mix_line, back_send, shape_send, back, shaped,
    lhs, cspec, gpart, gbuf, pbuf, rsbuf, fsum, fgpart, fgbuf,
    wsem, halo_send, halo_recv, a2a_send, a2a_recv,
    gp_send, gp_recv, ga_send, ga_recv, rs_send, rs_recv, fp_send, fp_recv, fa_send, fa_recv,
):
    a, d = lax.axis_index("lat"), lax.axis_index("lon")
    groups = lons // lats
    cols = field.shape[2]
    chans = lons * 8
    up, down = lax.rem(a + 1, lats), lax.rem(a + lats - 1, lats)
    east, west = lax.rem(d + 1, lons), lax.rem(d + lons - 1, lons)

    barrier = pltpu.get_barrier_semaphore()

    def greet(lat, lon):
        pl.semaphore_signal(barrier, inc=1, device_id=(lat, lon), device_id_type=MESH)

    def greet_lat(i, carry):
        greet(lax.rem(a + i, lats), d)
        return carry

    def greet_lon(i, carry):
        greet(a, lax.rem(d + i, lons))
        return carry

    lax.fori_loop(1, lats, greet_lat, 0)
    for lat in (up, down):
        for lon in (east, west):
            greet(lat, lon)
    lax.fori_loop(1, lons, greet_lon, 0)

    def send(src, dst, send_sem, recv_sem, lat, lon):
        copy = pltpu.make_async_remote_copy(
            src_ref=src, dst_ref=dst, send_sem=send_sem, recv_sem=recv_sem,
            device_id=(lat, lon), device_id_type=MESH,
        )
        copy.start()

    def await_bytes(ref, sem):
        pltpu.make_async_copy(ref, ref, sem).wait()

    def exchange(src, dst, index):
        def step(i, carry):
            peer = lax.rem(d + i, lons)
            send(src.at[peer], dst.at[d], a2a_send.at[index], a2a_recv.at[index], a, peer)
            return carry

        lax.fori_loop(1, lons, step, 0)

    def exchanged(src, dst, index):
        await_bytes(dst.at[pl.ds(0, lons - 1)], a2a_recv.at[index])
        dst[d] = src[d]

    def exchange_sent(src, index):
        await_bytes(src.at[pl.ds(0, lons - 1)], a2a_send.at[index])

    low, high = pl.ds(0, 8), pl.ds(cols + 8, 8)
    middle = pl.ds(8, cols)
    rows = [(up, 0), (down, 2)]
    edges = [(up, 0), (a, 1), (down, 2)]

    def halo_plan(ext, index):
        plan = []
        for lat, slot in rows:
            plan.append((ext.at[1, middle], ext.at[slot, middle], lat, d))
        for lat, slot in edges:
            plan.append((ext.at[1, pl.ds(8, 8)], ext.at[slot, high], lat, west))
            plan.append((ext.at[1, pl.ds(cols, 8)], ext.at[slot, low], lat, east))
        return [
            pltpu.make_async_remote_copy(
                src_ref=src, dst_ref=dst, send_sem=halo_send.at[index, i],
                recv_sem=halo_recv.at[index, i], device_id=(lat, lon), device_id_type=MESH,
            )
            for i, (src, dst, lat, lon) in enumerate(plan)
        ]

    wcopy = pltpu.make_async_copy(weight, wbuf, wsem)
    wcopy.start()
    xe[1, middle] = field[...].reshape(chans, cols).T

    pl.semaphore_wait(barrier, lats - 1 + lons - 1 + 4)

    field_halo = halo_plan(xe, 0)
    for copy in field_halo:
        copy.start()

    for h in range(groups):
        e = lax.rem(d + lats - a, lats) + lats * h

        @pl.when(e != d)
        def _():
            send(gain.at[:, e], gpart.at[d // lats], gp_send.at[h], gp_recv.at[d // lats], a, e)

        @pl.when(e == d)
        def _():
            gpart[d // lats] = gain[:, e]

    exchange(cot, cot_line, 0)

    wcopy.wait()
    for t in range(9):
        w_hi, w_lo = split(wbuf[t])
        block = slice(t * chans, (t + 1) * chans)
        wrow_hi[:, block] = w_hi
        wrow_lo[:, block] = w_lo
        wcol_hi[block, :] = w_hi
        wcol_lo[block, :] = w_lo

    gain_slot = lax.rem(a + d, lats)
    for g in range(groups):
        @pl.when(gain_slot + lats * g != d)
        def _():
            await_bytes(gpart.at[g], gp_recv.at[g])

    def gather_gain(i, carry):
        send(gpart, gbuf.at[gain_slot], ga_send, ga_recv, lax.rem(a + i, lats), d)
        return carry

    lax.fori_loop(1, lats, gather_gain, 0)

    def fill_windows(ext, backward):
        for slot in range(3):
            for s in range(3):
                t = (2 - slot if backward else slot) * 3 + s
                start = 9 - s if backward else 7 + s
                window = ext[slot, start : start + cols, :]
                if slot == 0:
                    window = jnp.where(a > 0, window, 0.0)
                if slot == 2:
                    window = jnp.where(a < lats - 1, window, 0.0)
                w_hi, w_lo = split(window)
                block = slice(t * chans, (t + 1) * chans)
                windows[0:cols, block] = w_hi
                windows[cols : 2 * cols, block] = w_lo

    for copy in field_halo:
        copy.wait_recv()
    fill_windows(xe, False)
    both = matmul(wrow_hi[...], windows[...], ((1,), (1,)))
    small = matmul(wrow_lo[...], windows[0:cols, :], ((1,), (1,)))
    mixed[...] = (both[:, :cols] + both[:, cols:] + small).reshape(lons, 8, cols)
    exchange(mixed, mix_line, 1)

    def transform(line):
        spec = real_forward([line[i] for i in range(lons)])
        for slot, r in enumerate(residues):
            re, im = spec[r] if 2 * r <= lons else conj(spec[lons - r])
            c, s = twiddle[0, slot : slot + 1, :], twiddle[1, slot : slot + 1, :]
            block = slice(slot * 8, slot * 8 + 8)
            if im is None:
                lhs[block, 0:cols] = re * c
                lhs[block, cols : 2 * cols] = -re * s
            else:
                lhs[block, 0:cols] = re * c + im * s
                lhs[block, cols : 2 * cols] = im * c - re * s
        hi, lo = split(lhs[...])
        dims = ((1,), (0,))
        full = matmul(hi, mats[0], dims) + matmul(hi, mats[1], dims) + matmul(lo, mats[0], dims)
        return full[:, :cols], full[:, cols:]

    def untransform(re, im, dst):
        hi, lo = split(jnp.concatenate([re, im], axis=1))
        dims = ((1,), (0,))
        lhs[...] = matmul(hi, mats[2], dims) + matmul(hi, mats[3], dims) + matmul(lo, mats[2], dims)
        turned = [None] * lons
        for slot, r in enumerate(residues):
            block = slice(slot * 8, slot * 8 + 8)
            c, s = twiddle[0, slot : slot + 1, :], twiddle[1, slot : slot + 1, :]
            re, im = lhs[block, 0:cols], lhs[block, cols : 2 * cols]
            turned[r] = (re * c - im * s, im * c + re * s)
        half = [(turned[0][0], None)]
        for r in range(1, lons // 2):
            half.append(tuple(0.5 * v for v in plus(turned[r], conj(turned[lons - r]))))
        half.append((turned[lons // 2][0], None))
        for i, value in enumerate(real_inverse(half)):
            dst[i] = value

    exchanged(cot, cot_line, 0)
    c_re, c_im = transform(cot_line)
    cspec[0] = c_re
    cspec[1] = c_im
    await_bytes(gbuf.at[pl.ds(0, lats - 1)], ga_recv)
    gbuf[gain_slot] = gpart[...]
    g_re = gbuf[:, :, 0].reshape(chans, cols)
    g_im = gbuf[:, :, 1].reshape(chans, cols)
    untransform(g_re * c_re + g_im * c_im, g_re * c_im - g_im * c_re, back_send)
    exchange(back_send, back, 2)

    exchanged(mixed, mix_line, 1)
    s_re, s_im = transform(mix_line)
    c_re, c_im = cspec[0], cspec[1]
    scale = 1.0 / (cols * lons)
    tiles = (lats, groups, 8, cols)
    pbuf[:, :, 0] = ((s_re * c_re + s_im * c_im) * scale).reshape(tiles)
    pbuf[:, :, 1] = ((s_re * c_im - s_im * c_re) * scale).reshape(tiles)

    def scatter_sums(i, carry):
        peer = lax.rem(a + i, lats)
        send(pbuf.at[lax.rem(peer + d, lats)], rsbuf.at[a], rs_send, rs_recv, peer, d)
        return carry

    lax.fori_loop(1, lats, scatter_sums, 0)

    g_re = gbuf[:, :, 0].reshape(chans, cols)
    g_im = gbuf[:, :, 1].reshape(chans, cols)
    untransform(g_re * s_re - g_im * s_im, g_re * s_im + g_im * s_re, shape_send)
    exchange(shape_send, shaped, 3)

    await_bytes(rsbuf.at[pl.ds(0, lats - 1)], rs_recv)
    rsbuf[a] = pbuf[gain_slot]
    fsum[...] = jnp.sum(rsbuf[...], axis=0)
    for h in range(groups):
        e = gain_slot + lats * h

        @pl.when(e != d)
        def _():
            send(fsum.at[h], fgpart.at[d // lats], fp_send.at[h], fp_recv.at[d // lats], a, e)

        @pl.when(e == d)
        def _():
            fgpart[d // lats] = fsum[h]

    exchanged(back_send, back, 2)
    be[1, middle] = back[...].reshape(chans, cols).T
    back_halo = halo_plan(be, 1)
    for copy in back_halo:
        copy.start()

    sum_slot = lax.rem(d + lats - a, lats)
    for g in range(groups):
        @pl.when(sum_slot + lats * g != d)
        def _():
            await_bytes(fgpart.at[g], fp_recv.at[g])

    def gather_sums(i, carry):
        send(fgpart, fgbuf.at[sum_slot], fa_send, fa_recv, lax.rem(a + i, lats), d)
        return carry

    lax.fori_loop(1, lats, gather_sums, 0)

    for copy in back_halo:
        copy.wait_recv()
    fill_windows(be, True)
    both = matmul(windows[...], wcol_hi[...], ((1,), (0,)))
    small = matmul(windows[0:cols, :], wcol_lo[...], ((1,), (0,)))
    grad = (both[:cols] + both[cols:] + small).T
    igrad[...] = cot[...] + grad.reshape(lons, 8, cols)

    await_bytes(fgbuf.at[pl.ds(0, lats - 1)], fa_recv)
    fgbuf[sum_slot] = fgpart[...]
    for i in range(lons):
        fgrad[:, i] = fgbuf[i % lats, i // lats]

    exchanged(shape_send, shaped, 3)
    out[...] = field[...] + shaped[...]

    for copy in field_halo + back_halo:
        copy.wait_send()
    for h in range(groups):
        @pl.when(lax.rem(d + lats - a, lats) + lats * h != d)
        def _():
            await_bytes(gpart.at[h], gp_send.at[h])

        @pl.when(gain_slot + lats * h != d)
        def _():
            await_bytes(fsum.at[h], fp_send.at[h])

    await_bytes(gbuf.at[pl.ds(0, lats - 1)], ga_send)
    await_bytes(rsbuf.at[pl.ds(0, lats - 1)], rs_send)
    await_bytes(fgbuf.at[pl.ds(0, lats - 1)], fa_send)
    for index, src in enumerate((cot, mixed, back_send, shape_send)):
        exchange_sent(src, index)


def solution(mesh):
    lats, lons = mesh.shape["lat"], mesh.shape["lon"]
    groups = lons // lats

    def on_device(field, cotangent, conv_weight, spectral_filter):
        chans, _, cols = field.shape
        residues, mats, twiddle = tables(lats, lons, cols)
        tiles = (lons, 8, cols)
        tile = jax.ShapeDtypeStruct(tiles, f32)
        vmem = pl.BlockSpec(memory_space=pltpu.VMEM)
        line = pltpu.VMEM(tiles, f32)
        dma = pltpu.SemaphoreType.DMA
        share = (groups, 2, 8, cols)
        shares = (lats,) + share
        out, igrad, fgrad = pl.pallas_call(
            functools.partial(layer_kernel, lats, lons, residues),
            out_shape=(tile, tile, jax.ShapeDtypeStruct((2,) + tiles, f32)),
            in_specs=[vmem, vmem, pl.BlockSpec(memory_space=pl.ANY), vmem, vmem, vmem],
            out_specs=(vmem, vmem, vmem),
            scratch_shapes=[
                pltpu.VMEM((9, chans, chans), f32),
                pltpu.VMEM((chans, 9 * chans), bf16),
                pltpu.VMEM((chans, 9 * chans), bf16),
                pltpu.VMEM((9 * chans, chans), bf16),
                pltpu.VMEM((9 * chans, chans), bf16),
                pltpu.VMEM((3, cols + 16, chans), f32),
                pltpu.VMEM((3, cols + 16, chans), f32),
                pltpu.VMEM((2 * cols, 9 * chans), bf16),
                line, line, line, line, line, line, line,
                pltpu.VMEM((chans, 2 * cols), f32),
                pltpu.VMEM((2, chans, cols), f32),
                pltpu.VMEM(share, f32),
                pltpu.VMEM(shares, f32),
                pltpu.VMEM(shares, f32),
                pltpu.VMEM(shares, f32),
                pltpu.VMEM(share, f32),
                pltpu.VMEM(share, f32),
                pltpu.VMEM(shares, f32),
                dma, dma((2, 8)), dma((2, 8)), dma((4,)), dma((4,)),
                dma((groups,)), dma((groups,)), dma, dma, dma, dma,
                dma((groups,)), dma((groups,)), dma, dma,
            ],
            compiler_params=pltpu.CompilerParams(
                collective_id=0, has_side_effects=True, vmem_limit_bytes=48 << 20
            ),
        )(
            field.reshape(tiles),
            cotangent.reshape(tiles),
            conv_weight.reshape(9, chans, chans),
            spectral_filter.reshape((2,) + tiles),
            jnp.asarray(mats),
            jnp.asarray(twiddle),
        )
        shape = (chans, 1, cols)
        return out.reshape(shape), igrad.reshape(shape), fgrad.reshape(2, chans, cols)

    placed = (P(None, "lat", "lon"), P(None, "lat", "lon"), P(), P(None, None, "lon"))
    return jax.shard_map(
        on_device,
        mesh=mesh,
        in_specs=placed,
        out_specs=(P(None, "lat", "lon"), P(None, "lat", "lon"), P(None, None, "lon")),
        check_vma=False,
    )
```

```python
import functools
import math

import jax
import jax.numpy as jnp
import ml_dtypes
import numpy as np
from jax import lax
from jax.experimental import pallas as pl
from jax.experimental.pallas import tpu as pltpu
from jax.sharding import PartitionSpec as P

MESH = pl.DeviceIdType.MESH
f32, bf16 = jnp.float32, jnp.bfloat16


def split(value):
    high = value.astype(bf16)
    return high, (value - high.astype(f32)).astype(bf16)


def matmul(lhs, rhs, dims):
    return lax.dot_general(lhs, rhs, (dims, ((), ())), preferred_element_type=f32)


def turn(value, angle):
    re, im = value
    c, s = math.cos(angle), math.sin(angle)
    return re * c - im * s, im * c + re * s


def conj(value):
    return value[0], None if value[1] is None else -value[1]


def plus(a, b):
    if a[1] is None or b[1] is None:
        return a[0] + b[0], a[1] if b[1] is None else b[1]
    return a[0] + b[0], a[1] + b[1]


def minus(a, b):
    if a[1] is None or b[1] is None:
        return a[0] - b[0], a[1] if b[1] is None else -b[1]
    return a[0] - b[0], a[1] - b[1]


def real_forward(xs):
    n = len(xs)
    if n == 1:
        return [(xs[0], None)]
    if n == 2:
        return [(xs[0] + xs[1], None), (xs[0] - xs[1], None)]
    even, odd = real_forward(xs[0::2]), real_forward(xs[1::2])
    out = [None] * (n // 2 + 1)
    for r in range(n // 4 + 1):
        e, o = even[r], odd[r]
        if r == 0:
            out[0], out[n // 2] = (e[0] + o[0], None), (e[0] - o[0], None)
        elif r == n // 4:
            out[r] = (e[0], -o[0])
        else:
            o = turn(o, -2 * math.pi * r / n)
            out[r], out[n // 2 - r] = plus(e, o), conj(minus(e, o))
    return out


def real_inverse(spec):
    n = 2 * (len(spec) - 1)
    if n == 2:
        a, b = spec[0][0], spec[1][0]
        return [a + b, a - b]
    even, odd = [None] * (n // 4 + 1), [None] * (n // 4 + 1)
    for r in range(n // 4 + 1):
        a, b = spec[r], spec[n // 2 - r]
        if r == 0:
            even[0], odd[0] = (a[0] + b[0], None), (a[0] - b[0], None)
        elif r == n // 4:
            even[r], odd[r] = (2.0 * a[0], None), (-2.0 * a[1], None)
        else:
            b = conj(b)
            even[r], odd[r] = plus(a, b), turn(minus(a, b), 2 * math.pi * r / n)
    out = [None] * n
    out[0::2], out[1::2] = real_inverse(even), real_inverse(odd)
    return out


def flipped_bits(place, extent):
    width = extent.bit_length() - 1
    return sum((place >> bit & 1) << (width - 1 - bit) for bit in range(width))


def tables(lats, lons, columns):
    groups = lons // lats
    residues = [flipped_bits(slot % groups * lats + slot // groups, lons) for slot in range(lons)]
    m = np.arange(columns)
    inner = 2 * np.pi * (np.outer(m, m) % columns) / columns
    c, s = np.cos(inner), np.sin(inner)
    forward = np.block([[c, -s], [s, c]])
    inverse = np.block([[c, s], [-s, c]]) / (columns * lons)
    mats = []
    for mat in (forward, inverse):
        high = mat.astype(np.float32).astype(ml_dtypes.bfloat16)
        mats += [high, (mat - high.astype(np.float64)).astype(ml_dtypes.bfloat16)]
    outer = 2 * np.pi * np.outer(residues, m) / (columns * lons)
    twiddle = np.stack([np.cos(outer), np.sin(outer)]).astype(np.float32)
    return residues, np.stack(mats), twiddle


def layer_kernel(
    lats, lons, residues,
    field_in, cot_in, weight_in, gain_in, mats_in, twiddle_in,
    out, igrad, fgrad,
    field, cot, gain, mats, twiddle, wbuf, wrow_hi, wrow_lo, wcol_hi, wcol_lo, xe, be, windows,
    mixed, cot_line, mix_line, back_send, shape_send, back, shaped,
    lhs, cspec, gpart, gbuf, pbuf, rsbuf, fsum, fgpart, fgbuf,
    load_sem, halo_send, halo_recv, a2a_send, a2a_recv,
    gp_send, gp_recv, ga_send, ga_recv, rs_send, rs_recv, fp_send, fp_recv, fa_send, fa_recv,
):
    a, d = lax.axis_index("lat"), lax.axis_index("lon")
    groups = lons // lats
    cols = field.shape[2]
    chans = lons * 8
    ring = lons // 2

    loads = [
        pltpu.make_async_copy(src, dst, load_sem.at[i])
        for i, (src, dst) in enumerate(
            [(field_in, field), (cot_in, cot), (gain_in, gain), (weight_in, wbuf), (twiddle_in, twiddle), (mats_in, mats)]
        )
    ]
    for load in loads:
        load.start()

    def far_first(u):
        away = ring // 2 - (u + 2) // 4
        away = jnp.where(lax.rem((u + 2) // 2, 2) == 1, ring - away, away)
        half = lax.rem(d // ring + 1 - lax.rem(u, 2), 2)
        return half * ring + lax.rem(d + away, ring)
    up, down = lax.rem(a + 1, lats), lax.rem(a + lats - 1, lats)
    east, west = lax.rem(d + 1, lons), lax.rem(d + lons - 1, lons)

    barrier = pltpu.get_barrier_semaphore()

    def greet(lat, lon):
        pl.semaphore_signal(barrier, inc=1, device_id=(lat, lon), device_id_type=MESH)

    def greet_lat(i, carry):
        greet(lax.rem(a + i, lats), d)
        return carry

    def greet_lon(i, carry):
        greet(a, far_first(i))
        return carry

    lax.fori_loop(0, lons - 1, greet_lon, 0)
    lax.fori_loop(1, lats, greet_lat, 0)
    for lat in (up, down):
        for lon in (east, west):
            greet(lat, lon)

    def send(src, dst, send_sem, recv_sem, lat, lon):
        copy = pltpu.make_async_remote_copy(
            src_ref=src, dst_ref=dst, send_sem=send_sem, recv_sem=recv_sem,
            device_id=(lat, lon), device_id_type=MESH,
        )
        copy.start()

    def await_bytes(ref, sem):
        pltpu.make_async_copy(ref, ref, sem).wait()

    def exchange(src, dst, index):
        def step(i, carry):
            peer = far_first(i)
            send(src.at[peer], dst.at[d], a2a_send.at[index], a2a_recv.at[index], a, peer)
            return carry

        lax.fori_loop(0, lons - 1, step, 0)

    def exchanged(src, dst, index):
        await_bytes(dst.at[pl.ds(0, lons - 1)], a2a_recv.at[index])
        dst[d] = src[d]

    def exchange_sent(src, index):
        await_bytes(src.at[pl.ds(0, lons - 1)], a2a_send.at[index])

    low, high = pl.ds(0, 8), pl.ds(cols + 8, 8)
    middle = pl.ds(8, cols)
    rows = [(up, 0), (down, 2)]
    edges = [(up, 0), (a, 1), (down, 2)]

    def halo_plan(ext, index):
        plan = []
        for lat, slot in rows:
            plan.append((ext.at[1, middle], ext.at[slot, middle], lat, d))
        for lat, slot in edges:
            plan.append((ext.at[1, pl.ds(8, 8)], ext.at[slot, high], lat, west))
            plan.append((ext.at[1, pl.ds(cols, 8)], ext.at[slot, low], lat, east))
        return [
            pltpu.make_async_remote_copy(
                src_ref=src, dst_ref=dst, send_sem=halo_send.at[index, i],
                recv_sem=halo_recv.at[index, i], device_id=(lat, lon), device_id_type=MESH,
            )
            for i, (src, dst, lat, lon) in enumerate(plan)
        ]

    loads[0].wait()
    xe[1, middle] = field[...].reshape(chans, cols).T
    loads[1].wait()
    loads[2].wait()

    pl.semaphore_wait(barrier, lats - 1 + lons - 1 + 4)

    for h in range(groups):
        e = lax.rem(d + lats - a, lats) + lats * h

        @pl.when(e != d)
        def _():
            send(gain.at[:, e], gpart.at[d // lats], gp_send.at[h], gp_recv.at[d // lats], a, e)

        @pl.when(e == d)
        def _():
            gpart[d // lats] = gain[:, e]

    field_halo = halo_plan(xe, 0)
    for copy in field_halo:
        copy.start()

    exchange(cot, cot_line, 0)

    loads[3].wait()
    for t in range(9):
        w_hi, w_lo = split(wbuf[t])
        block = slice(t * chans, (t + 1) * chans)
        wrow_hi[:, block] = w_hi
        wrow_lo[:, block] = w_lo
        wcol_hi[block, :] = w_hi
        wcol_lo[block, :] = w_lo

    def fill_windows(ext, slot, backward):
        for s in range(3):
            t = (2 - slot if backward else slot) * 3 + s
            start = 9 - s if backward else 7 + s
            window = ext[slot, start : start + cols, :]
            if slot == 0:
                window = jnp.where(a > 0, window, 0.0)
            if slot == 2:
                window = jnp.where(a < lats - 1, window, 0.0)
            w_hi, w_lo = split(window)
            block = slice(t * chans, (t + 1) * chans)
            windows[0:cols, block] = w_hi
            windows[cols : 2 * cols, block] = w_lo

    def halo_arrived(plan, slot):
        for i in {0: (0, 2, 3), 1: (4, 5), 2: (1, 6, 7)}[slot]:
            plan[i].wait_recv()

    def taps(slot, backward):
        first = 2 - slot if backward else slot
        return slice(first * 3 * chans, (first * 3 + 3) * chans)

    gain_slot = lax.rem(a + d, lats)

    def forward_gain():
        for g in range(groups):
            @pl.when(gain_slot + lats * g != d)
            def _():
                await_bytes(gpart.at[g], gp_recv.at[g])

        def gather_gain(i, carry):
            send(gpart, gbuf.at[gain_slot], ga_send, ga_recv, lax.rem(a + i, lats), d)
            return carry

        lax.fori_loop(1, lats, gather_gain, 0)

    halves = []
    for slot in (1, 0, 2):
        halo_arrived(field_halo, slot)
        fill_windows(xe, slot, False)
        block = taps(slot, False)
        halves.append(
            (
                matmul(wrow_hi[:, block], windows[:, block], ((1,), (1,))),
                matmul(wrow_lo[:, block], windows[0:cols, block], ((1,), (1,))),
            )
        )
    both = halves[0][0] + halves[1][0] + halves[2][0]
    small = halves[0][1] + halves[1][1] + halves[2][1]
    mixed[...] = (both[:, :cols] + both[:, cols:] + small).reshape(lons, 8, cols)
    exchange(mixed, mix_line, 1)
    forward_gain()

    def transform(line):
        spec = real_forward([line[i] for i in range(lons)])
        for slot, r in enumerate(residues):
            re, im = spec[r] if 2 * r <= lons else conj(spec[lons - r])
            c, s = twiddle[0, slot : slot + 1, :], twiddle[1, slot : slot + 1, :]
            block = slice(slot * 8, slot * 8 + 8)
            if im is None:
                lhs[block, 0:cols] = re * c
                lhs[block, cols : 2 * cols] = -re * s
            else:
                lhs[block, 0:cols] = re * c + im * s
                lhs[block, cols : 2 * cols] = im * c - re * s
        hi, lo = split(lhs[...])
        dims = ((1,), (0,))
        full = matmul(hi, mats[0], dims) + matmul(hi, mats[1], dims) + matmul(lo, mats[0], dims)
        return full[:, :cols], full[:, cols:]

    def untransform(re, im, dst):
        hi, lo = split(jnp.concatenate([re, im], axis=1))
        dims = ((1,), (0,))
        lhs[...] = matmul(hi, mats[2], dims) + matmul(hi, mats[3], dims) + matmul(lo, mats[2], dims)
        turned = [None] * lons
        for slot, r in enumerate(residues):
            block = slice(slot * 8, slot * 8 + 8)
            c, s = twiddle[0, slot : slot + 1, :], twiddle[1, slot : slot + 1, :]
            re, im = lhs[block, 0:cols], lhs[block, cols : 2 * cols]
            turned[r] = (re * c - im * s, im * c + re * s)
        half = [(turned[0][0], None)]
        for r in range(1, lons // 2):
            half.append(tuple(0.5 * v for v in plus(turned[r], conj(turned[lons - r]))))
        half.append((turned[lons // 2][0], None))
        for i, value in enumerate(real_inverse(half)):
            dst[i] = value

    loads[4].wait()
    loads[5].wait()
    exchanged(cot, cot_line, 0)
    c_re, c_im = transform(cot_line)
    cspec[0] = c_re
    cspec[1] = c_im
    await_bytes(gbuf.at[pl.ds(0, lats - 1)], ga_recv)
    gbuf[gain_slot] = gpart[...]
    g_re = gbuf[:, :, 0].reshape(chans, cols)
    g_im = gbuf[:, :, 1].reshape(chans, cols)
    untransform(g_re * c_re + g_im * c_im, g_re * c_im - g_im * c_re, back_send)
    exchange(back_send, back, 2)

    exchanged(mixed, mix_line, 1)
    s_re, s_im = transform(mix_line)
    c_re, c_im = cspec[0], cspec[1]
    scale = 1.0 / (cols * lons)
    tiles = (lats, groups, 8, cols)
    pbuf[:, :, 0] = ((s_re * c_re + s_im * c_im) * scale).reshape(tiles)
    pbuf[:, :, 1] = ((s_re * c_im - s_im * c_re) * scale).reshape(tiles)

    def scatter_sums(i, carry):
        peer = lax.rem(a + i, lats)
        send(pbuf.at[lax.rem(peer + d, lats)], rsbuf.at[a], rs_send, rs_recv, peer, d)
        return carry

    lax.fori_loop(1, lats, scatter_sums, 0)

    g_re = gbuf[:, :, 0].reshape(chans, cols)
    g_im = gbuf[:, :, 1].reshape(chans, cols)
    untransform(g_re * s_re - g_im * s_im, g_re * s_im + g_im * s_re, shape_send)
    exchange(shape_send, shaped, 3)

    await_bytes(rsbuf.at[pl.ds(0, lats - 1)], rs_recv)
    rsbuf[a] = pbuf[gain_slot]
    fsum[...] = jnp.sum(rsbuf[...], axis=0)
    for h in range(groups):
        e = gain_slot + lats * h

        @pl.when(e != d)
        def _():
            send(fsum.at[h], fgpart.at[d // lats], fp_send.at[h], fp_recv.at[d // lats], a, e)

        @pl.when(e == d)
        def _():
            fgpart[d // lats] = fsum[h]

    exchanged(back_send, back, 2)
    be[1, middle] = back[...].reshape(chans, cols).T
    back_halo = halo_plan(be, 1)
    for copy in back_halo:
        copy.start()

    sum_slot = lax.rem(d + lats - a, lats)

    def forward_sums():
        for g in range(groups):
            @pl.when(sum_slot + lats * g != d)
            def _():
                await_bytes(fgpart.at[g], fp_recv.at[g])

        def gather_sums(i, carry):
            send(fgpart, fgbuf.at[sum_slot], fa_send, fa_recv, lax.rem(a + i, lats), d)
            return carry

        lax.fori_loop(1, lats, gather_sums, 0)

    halves = []
    for slot in (1, 0, 2):
        halo_arrived(back_halo, slot)
        fill_windows(be, slot, True)
        block = taps(slot, True)
        halves.append(
            (
                matmul(windows[:, block], wcol_hi[block, :], ((1,), (0,))),
                matmul(windows[0:cols, block], wcol_lo[block, :], ((1,), (0,))),
            )
        )
        if slot == 1:
            forward_sums()
    both = halves[0][0] + halves[1][0] + halves[2][0]
    small = halves[0][1] + halves[1][1] + halves[2][1]
    grad = (both[:cols] + both[cols:] + small).T
    igrad[...] = cot[...] + grad.reshape(lons, 8, cols)

    exchanged(shape_send, shaped, 3)
    out[...] = field[...] + shaped[...]

    await_bytes(fgbuf.at[pl.ds(0, lats - 1)], fa_recv)
    fgbuf[sum_slot] = fgpart[...]
    for i in range(lons):
        fgrad[:, i] = fgbuf[i % lats, i // lats]

    for copy in field_halo + back_halo:
        copy.wait_send()
    for h in range(groups):
        @pl.when(lax.rem(d + lats - a, lats) + lats * h != d)
        def _():
            await_bytes(gpart.at[h], gp_send.at[h])

        @pl.when(gain_slot + lats * h != d)
        def _():
            await_bytes(fsum.at[h], fp_send.at[h])

    await_bytes(gbuf.at[pl.ds(0, lats - 1)], ga_send)
    await_bytes(rsbuf.at[pl.ds(0, lats - 1)], rs_send)
    await_bytes(fgbuf.at[pl.ds(0, lats - 1)], fa_send)
    for index, src in enumerate((cot, mixed, back_send, shape_send)):
        exchange_sent(src, index)


def store_kernel(*refs):
    sources, results, sems = refs[:3], refs[3:6], refs[6]
    copies = [
        pltpu.make_async_copy(src, dst, sems.at[i])
        for i, (src, dst) in enumerate(zip(sources, results))
    ]
    for copy in copies:
        copy.start()
    for copy in copies:
        copy.wait()


def solution(mesh):
    lats, lons = mesh.shape["lat"], mesh.shape["lon"]
    groups = lons // lats

    def on_device(field, cotangent, conv_weight, spectral_filter):
        chans, _, cols = field.shape
        residues, mats, twiddle = tables(lats, lons, cols)
        tiles = (lons, 8, cols)
        tile = jax.ShapeDtypeStruct(tiles, f32)
        vmem = pl.BlockSpec(memory_space=pltpu.VMEM)
        line = pltpu.VMEM(tiles, f32)
        dma = pltpu.SemaphoreType.DMA
        share = (groups, 2, 8, cols)
        shares = (lats,) + share
        out, igrad, fgrad = pl.pallas_call(
            functools.partial(layer_kernel, lats, lons, residues),
            out_shape=(tile, tile, jax.ShapeDtypeStruct((2,) + tiles, f32)),
            in_specs=[pl.BlockSpec(memory_space=pltpu.HBM)] * 6,
            out_specs=(vmem, vmem, vmem),
            scratch_shapes=[
                line, line,
                pltpu.VMEM((2,) + tiles, f32),
                pltpu.VMEM(mats.shape, bf16),
                pltpu.VMEM(twiddle.shape, f32),
                pltpu.VMEM((9, chans, chans), f32),
                pltpu.VMEM((chans, 9 * chans), bf16),
                pltpu.VMEM((chans, 9 * chans), bf16),
                pltpu.VMEM((9 * chans, chans), bf16),
                pltpu.VMEM((9 * chans, chans), bf16),
                pltpu.VMEM((3, cols + 16, chans), f32),
                pltpu.VMEM((3, cols + 16, chans), f32),
                pltpu.VMEM((2 * cols, 9 * chans), bf16),
                line, line, line, line, line, line, line,
                pltpu.VMEM((chans, 2 * cols), f32),
                pltpu.VMEM((2, chans, cols), f32),
                pltpu.VMEM(share, f32),
                pltpu.VMEM(shares, f32),
                pltpu.VMEM(shares, f32),
                pltpu.VMEM(shares, f32),
                pltpu.VMEM(share, f32),
                pltpu.VMEM(share, f32),
                pltpu.VMEM(shares, f32),
                dma((6,)), dma((2, 8)), dma((2, 8)), dma((4,)), dma((4,)),
                dma((groups,)), dma((groups,)), dma, dma, dma, dma,
                dma((groups,)), dma((groups,)), dma, dma,
            ],
            compiler_params=pltpu.CompilerParams(
                collective_id=0, has_side_effects=True, vmem_limit_bytes=40 << 20
            ),
        )(
            *(
                pltpu.with_memory_space_constraint(v, pltpu.HBM)
                for v in (
                    field.reshape(tiles),
                    cotangent.reshape(tiles),
                    conv_weight.reshape(9, chans, chans),
                    spectral_filter.reshape((2,) + tiles),
                    jnp.asarray(mats),
                    jnp.asarray(twiddle),
                )
            )
        )
        anywhere = pl.BlockSpec(memory_space=pl.ANY)
        out, igrad, fgrad = pl.pallas_call(
            store_kernel,
            out_shape=tuple(jax.ShapeDtypeStruct(v.shape, f32) for v in (out, igrad, fgrad)),
            in_specs=[vmem] * 3,
            out_specs=(anywhere,) * 3,
            scratch_shapes=[dma((3,))],
            compiler_params=pltpu.CompilerParams(has_side_effects=True),
        )(*(pltpu.with_memory_space_constraint(v, pltpu.VMEM) for v in (out, igrad, fgrad)))
        shape = (chans, 1, cols)
        return out.reshape(shape), igrad.reshape(shape), fgrad.reshape(2, chans, cols)

    placed = (P(None, "lat", "lon"), P(None, "lat", "lon"), P(), P(None, None, "lon"))
    return jax.shard_map(
        on_device,
        mesh=mesh,
        in_specs=placed,
        out_specs=(P(None, "lat", "lon"), P(None, "lat", "lon"), P(None, None, "lon")),
        check_vma=False,
    )
```

```python
import functools
import math

import jax
import jax.numpy as jnp
import ml_dtypes
import numpy as np
from jax import lax
from jax.experimental import pallas as pl
from jax.experimental.pallas import tpu as pltpu
from jax.sharding import PartitionSpec as P

MESH = pl.DeviceIdType.MESH
f32, bf16 = jnp.float32, jnp.bfloat16


def split(value):
    high = value.astype(bf16)
    return high, (value - high.astype(f32)).astype(bf16)


def matmul(lhs, rhs, dims):
    return lax.dot_general(lhs, rhs, (dims, ((), ())), preferred_element_type=f32)


def turn(value, angle):
    re, im = value
    c, s = math.cos(angle), math.sin(angle)
    return re * c - im * s, im * c + re * s


def conj(value):
    return value[0], None if value[1] is None else -value[1]


def plus(a, b):
    if a[1] is None or b[1] is None:
        return a[0] + b[0], a[1] if b[1] is None else b[1]
    return a[0] + b[0], a[1] + b[1]


def minus(a, b):
    if a[1] is None or b[1] is None:
        return a[0] - b[0], a[1] if b[1] is None else -b[1]
    return a[0] - b[0], a[1] - b[1]


def real_forward(xs):
    n = len(xs)
    if n == 1:
        return [(xs[0], None)]
    if n == 2:
        return [(xs[0] + xs[1], None), (xs[0] - xs[1], None)]
    even, odd = real_forward(xs[0::2]), real_forward(xs[1::2])
    out = [None] * (n // 2 + 1)
    for r in range(n // 4 + 1):
        e, o = even[r], odd[r]
        if r == 0:
            out[0], out[n // 2] = (e[0] + o[0], None), (e[0] - o[0], None)
        elif r == n // 4:
            out[r] = (e[0], -o[0])
        else:
            o = turn(o, -2 * math.pi * r / n)
            out[r], out[n // 2 - r] = plus(e, o), conj(minus(e, o))
    return out


def real_inverse(spec):
    n = 2 * (len(spec) - 1)
    if n == 2:
        a, b = spec[0][0], spec[1][0]
        return [a + b, a - b]
    even, odd = [None] * (n // 4 + 1), [None] * (n // 4 + 1)
    for r in range(n // 4 + 1):
        a, b = spec[r], spec[n // 2 - r]
        if r == 0:
            even[0], odd[0] = (a[0] + b[0], None), (a[0] - b[0], None)
        elif r == n // 4:
            even[r], odd[r] = (2.0 * a[0], None), (-2.0 * a[1], None)
        else:
            b = conj(b)
            even[r], odd[r] = plus(a, b), turn(minus(a, b), 2 * math.pi * r / n)
    out = [None] * n
    out[0::2], out[1::2] = real_inverse(even), real_inverse(odd)
    return out


def flipped_bits(place, extent):
    width = extent.bit_length() - 1
    return sum((place >> bit & 1) << (width - 1 - bit) for bit in range(width))


def tables(lats, lons, columns):
    groups = lons // lats
    residues = [flipped_bits(slot % groups * lats + slot // groups, lons) for slot in range(lons)]
    m = np.arange(columns)
    inner = 2 * np.pi * (np.outer(m, m) % columns) / columns
    c, s = np.cos(inner), np.sin(inner)
    forward = np.block([[c, -s], [s, c]])
    inverse = np.block([[c, s], [-s, c]]) / (columns * lons)
    mats = []
    for mat in (forward, inverse):
        high = mat.astype(np.float32).astype(ml_dtypes.bfloat16)
        mats += [high, (mat - high.astype(np.float64)).astype(ml_dtypes.bfloat16)]
    outer = 2 * np.pi * np.outer(residues, m) / (columns * lons)
    twiddle = np.stack([np.cos(outer), np.sin(outer)]).astype(np.float32)
    return residues, np.stack(mats), twiddle


def layer_kernel(
    lats, lons, residues,
    field_in, cot_in, weight_in, gain_in, mats_in, twiddle_in,
    out, igrad, fgrad,
    field, cot, gain, mats, twiddle, wbuf, wrow_hi, wrow_lo, wcol_hi, wcol_lo, xe, be, windows,
    mixed, cot_line, mix_line, back_send, shape_send, back, shaped,
    lhs, cspec, gpart, gbuf, pbuf, rsbuf, fsum, fgpart, fgbuf,
    load_sem, halo_send, halo_recv, a2a_send, a2a_recv,
    gp_send, gp_recv, ga_send, ga_recv, rs_send, rs_recv, fp_send, fp_recv, fa_send, fa_recv,
):
    a, d = lax.axis_index("lat"), lax.axis_index("lon")
    groups = lons // lats
    cols = field.shape[2]
    chans = lons * 8
    ring = lons // 2

    def far_first(u):
        away = ring // 2 - (u + 2) // 4
        away = jnp.where(lax.rem((u + 2) // 2, 2) == 1, ring - away, away)
        half = lax.rem(d // ring + 1 - lax.rem(u, 2), 2)
        return half * ring + lax.rem(d + away, ring)
    up, down = lax.rem(a + 1, lats), lax.rem(a + lats - 1, lats)
    east, west = lax.rem(d + 1, lons), lax.rem(d + lons - 1, lons)

    def far_lat(v):
        ys = lats // 4
        u = v // 4
        y = jnp.where(u == 0, 2, jnp.where(u == 1, 1, jnp.where(u == 2, 3, 0)))
        x = lax.rem(a // (2 * ys) + 1 - lax.rem(v // 2, 2), 2)
        y = lax.rem(lax.rem(a // 2, ys) + y, ys)
        return (x * ys + y) * 2 + lax.rem(a + 1 - lax.rem(v, 2), 2)

    barrier = pltpu.get_barrier_semaphore()

    def greet(lat, lon):
        pl.semaphore_signal(barrier, inc=1, device_id=(lat, lon), device_id_type=MESH)

    def greet_lat(i, carry):
        greet(lax.rem(a + i, lats), d)
        return carry

    def greet_lon(i, carry):
        greet(a, far_first(i))
        return carry

    lax.fori_loop(0, lons - 1, greet_lon, 0)
    lax.fori_loop(1, lats, greet_lat, 0)
    for lat in (up, down):
        for lon in (east, west):
            greet(lat, lon)

    loads = [
        pltpu.make_async_copy(src, dst, load_sem.at[i])
        for i, (src, dst) in enumerate(
            [(field_in, field), (cot_in, cot), (gain_in, gain), (weight_in, wbuf), (twiddle_in, twiddle), (mats_in, mats)]
        )
    ]
    for load in loads:
        load.start()

    def send(src, dst, send_sem, recv_sem, lat, lon):
        copy = pltpu.make_async_remote_copy(
            src_ref=src, dst_ref=dst, send_sem=send_sem, recv_sem=recv_sem,
            device_id=(lat, lon), device_id_type=MESH,
        )
        copy.start()

    def await_bytes(ref, sem):
        pltpu.make_async_copy(ref, ref, sem).wait()

    def share_of(row):
        return lax.rem(row + lats - lax.rem(d, lats), lats)

    def exchange(src, dst, index):
        def step(i, carry):
            peer = far_first(i)
            send(src.at[peer], dst.at[d], a2a_send.at[index], a2a_recv.at[index], a, peer)
            return carry

        lax.fori_loop(0, lons - 1, step, 0)

    def exchanged(src, dst, index):
        await_bytes(dst.at[pl.ds(0, lons - 1)], a2a_recv.at[index])
        dst[d] = src[d]

    def exchange_sent(src, index):
        await_bytes(src.at[pl.ds(0, lons - 1)], a2a_send.at[index])

    low, high = pl.ds(0, 8), pl.ds(cols + 8, 8)
    middle = pl.ds(8, cols)
    rows = [(up, 0), (down, 2)]
    edges = [(up, 0), (a, 1), (down, 2)]

    def halo_plan(ext, index):
        plan = []
        for lat, slot in rows:
            plan.append((ext.at[1, middle], ext.at[slot, middle], lat, d))
        for lat, slot in edges:
            plan.append((ext.at[1, pl.ds(8, 8)], ext.at[slot, high], lat, west))
            plan.append((ext.at[1, pl.ds(cols, 8)], ext.at[slot, low], lat, east))
        return [
            pltpu.make_async_remote_copy(
                src_ref=src, dst_ref=dst, send_sem=halo_send.at[index, i],
                recv_sem=halo_recv.at[index, i], device_id=(lat, lon), device_id_type=MESH,
            )
            for i, (src, dst, lat, lon) in enumerate(plan)
        ]

    loads[0].wait()
    xe[1, middle] = field[...].reshape(chans, cols).T
    loads[1].wait()
    loads[2].wait()

    pl.semaphore_wait(barrier, lats - 1 + lons - 1 + 4)

    for h in range(groups):
        e = share_of(a) + lats * h

        @pl.when(e != d)
        def _():
            send(gain.at[:, e], gpart.at[d // lats], gp_send.at[h], gp_recv.at[d // lats], a, e)

        @pl.when(e == d)
        def _():
            gpart[d // lats] = gain[:, e]

    field_halo = halo_plan(xe, 0)
    for copy in field_halo:
        copy.start()

    exchange(cot, cot_line, 0)

    loads[3].wait()
    for t in range(9):
        w_hi, w_lo = split(wbuf[t])
        block = slice(t * chans, (t + 1) * chans)
        wrow_hi[:, block] = w_hi
        wrow_lo[:, block] = w_lo
        wcol_hi[block, :] = w_hi
        wcol_lo[block, :] = w_lo

    def fill_windows(ext, slot, backward):
        for s in range(3):
            t = (2 - slot if backward else slot) * 3 + s
            start = 9 - s if backward else 7 + s
            window = ext[slot, start : start + cols, :]
            if slot == 0:
                window = jnp.where(a > 0, window, 0.0)
            if slot == 2:
                window = jnp.where(a < lats - 1, window, 0.0)
            w_hi, w_lo = split(window)
            block = slice(t * chans, (t + 1) * chans)
            windows[0:cols, block] = w_hi
            windows[cols : 2 * cols, block] = w_lo

    def halo_arrived(plan, slot):
        for i in {0: (0, 2, 3), 1: (4, 5), 2: (1, 6, 7)}[slot]:
            plan[i].wait_recv()

    def taps(slot, backward):
        first = 2 - slot if backward else slot
        return slice(first * 3 * chans, (first * 3 + 3) * chans)

    gain_slot = share_of(a)
    own_share = share_of(a)

    def forward_gain():
        for i in range(groups):
            g = lax.rem(d // lats + i, groups)

            @pl.when(gain_slot + lats * g != d)
            def _():
                await_bytes(gpart.at[g], gp_recv.at[g])

            def gather_gain(i, carry):
                send(gpart.at[g], gbuf.at[gain_slot, g], ga_send, ga_recv, far_lat(i), d)
                return carry

            lax.fori_loop(0, lats - 1, gather_gain, 0)

    halves = []
    for slot in (1, 0, 2):
        halo_arrived(field_halo, slot)
        fill_windows(xe, slot, False)
        block = taps(slot, False)
        halves.append(
            (
                matmul(wrow_hi[:, block], windows[:, block], ((1,), (1,))),
                matmul(wrow_lo[:, block], windows[0:cols, block], ((1,), (1,))),
            )
        )
    both = halves[0][0] + halves[1][0] + halves[2][0]
    small = halves[0][1] + halves[1][1] + halves[2][1]
    mixed[...] = (both[:, :cols] + both[:, cols:] + small).reshape(lons, 8, cols)
    exchange(mixed, mix_line, 1)
    forward_gain()

    def transform(line):
        spec = real_forward([line[i] for i in range(lons)])
        for slot, r in enumerate(residues):
            re, im = spec[r] if 2 * r <= lons else conj(spec[lons - r])
            c, s = twiddle[0, slot : slot + 1, :], twiddle[1, slot : slot + 1, :]
            block = slice(slot * 8, slot * 8 + 8)
            if im is None:
                lhs[block, 0:cols] = re * c
                lhs[block, cols : 2 * cols] = -re * s
            else:
                lhs[block, 0:cols] = re * c + im * s
                lhs[block, cols : 2 * cols] = im * c - re * s
        hi, lo = split(lhs[...])
        dims = ((1,), (0,))
        full = matmul(hi, mats[0], dims) + matmul(hi, mats[1], dims) + matmul(lo, mats[0], dims)
        return full[:, :cols], full[:, cols:]

    def untransform(re, im, dst):
        hi, lo = split(jnp.concatenate([re, im], axis=1))
        dims = ((1,), (0,))
        lhs[...] = matmul(hi, mats[2], dims) + matmul(hi, mats[3], dims) + matmul(lo, mats[2], dims)
        turned = [None] * lons
        for slot, r in enumerate(residues):
            block = slice(slot * 8, slot * 8 + 8)
            c, s = twiddle[0, slot : slot + 1, :], twiddle[1, slot : slot + 1, :]
            re, im = lhs[block, 0:cols], lhs[block, cols : 2 * cols]
            turned[r] = (re * c - im * s, im * c + re * s)
        half = [(turned[0][0], None)]
        for r in range(1, lons // 2):
            half.append(tuple(0.5 * v for v in plus(turned[r], conj(turned[lons - r]))))
        half.append((turned[lons // 2][0], None))
        for i, value in enumerate(real_inverse(half)):
            dst[i] = value

    loads[4].wait()
    loads[5].wait()
    exchanged(cot, cot_line, 0)
    c_re, c_im = transform(cot_line)
    cspec[0] = c_re
    cspec[1] = c_im
    await_bytes(gbuf.at[pl.ds(0, lats - 1)], ga_recv)
    gbuf[gain_slot] = gpart[...]
    g_re = gbuf[:, :, 0].reshape(chans, cols)
    g_im = gbuf[:, :, 1].reshape(chans, cols)
    untransform(g_re * c_re + g_im * c_im, g_re * c_im - g_im * c_re, back_send)
    exchange(back_send, back, 2)

    exchanged(mixed, mix_line, 1)
    s_re, s_im = transform(mix_line)
    c_re, c_im = cspec[0], cspec[1]
    scale = 1.0 / (cols * lons)
    for slot, r in enumerate(residues):
        if r <= lats:
            block = slice(slot * 8, slot * 8 + 8)
            pbuf[r, 0] = (s_re[block] * c_re[block] + s_im[block] * c_im[block]) * scale
            pbuf[r, 1] = (s_re[block] * c_im[block] - s_im[block] * c_re[block]) * scale

    def scatter_sums(i, carry):
        peer = far_lat(i)
        share = share_of(peer)
        send(pbuf.at[share], rsbuf.at[0, a], rs_send.at[0], rs_recv.at[0], peer, d)

        @pl.when(share == 0)
        def _():
            send(pbuf.at[lats], rsbuf.at[1, a], rs_send.at[1], rs_recv.at[1], peer, d)

        return carry

    lax.fori_loop(0, lats - 1, scatter_sums, 0)

    g_re = gbuf[:, :, 0].reshape(chans, cols)
    g_im = gbuf[:, :, 1].reshape(chans, cols)
    untransform(g_re * s_re - g_im * s_im, g_re * s_im + g_im * s_re, shape_send)
    exchange(shape_send, shaped, 3)

    await_bytes(rsbuf.at[0, pl.ds(0, lats - 1)], rs_recv.at[0])
    rsbuf[0, a] = pbuf[own_share]
    fsum[0] = jnp.sum(rsbuf[0], axis=0)

    @pl.when(own_share == 0)
    def _():
        await_bytes(rsbuf.at[1, pl.ds(0, lats - 1)], rs_recv.at[1])
        rsbuf[1, a] = pbuf[lats]
        fsum[1] = jnp.sum(rsbuf[1], axis=0)

    @pl.when(own_share > 0)
    def _():
        value = fsum[0].reshape(16, cols)
        first, rest = split(value)
        second, third = split(value - first.astype(f32) - rest.astype(f32))
        place = lax.broadcasted_iota(jnp.int32, (cols, cols), 0)
        other = lax.broadcasted_iota(jnp.int32, (cols, cols), 1)
        mirror = jnp.where(place + other == cols - 1, 1.0, 0.0).astype(bf16)
        parts = [matmul(part, mirror, ((1,), (0,))) for part in (first, rest, second)]
        value = (parts[0] + parts[1] + parts[2]).reshape(2, 8, cols)
        fsum[1, 0] = value[0]
        fsum[1, 1] = -value[1]

    def owner_of(residue):
        width = lons.bit_length() - 1
        return sum(lax.rem(residue // 2**bit, 2) * 2 ** (width - 1 - bit) for bit in range(width))

    owners = [owner_of(own_share), owner_of(jnp.where(own_share == 0, lats, lons - own_share))]
    for h, e in enumerate(owners):
        @pl.when(e != d)
        def _():
            send(fsum.at[h], fgpart.at[d // lats], fp_send.at[h], fp_recv.at[d // lats], a, e)

        @pl.when(e == d)
        def _():
            fgpart[d // lats] = fsum[h]

    exchanged(back_send, back, 2)
    be[1, middle] = back[...].reshape(chans, cols).T
    back_halo = halo_plan(be, 1)
    for copy in back_halo:
        copy.start()

    residue = owner_of(d)
    group = jnp.where(residue < lats, residue, lax.rem(lons - residue, lats))
    sum_slot = lax.rem(a + lats - group, lats)

    def forward_sums():
        for i in range(groups):
            g = lax.rem(d // lats + i, groups)

            @pl.when(sum_slot + lats * g != d)
            def _():
                await_bytes(fgpart.at[g], fp_recv.at[g])

            def gather_sums(i, carry):
                send(fgpart.at[g], fgbuf.at[sum_slot, g], fa_send, fa_recv, far_lat(i), d)
                return carry

            lax.fori_loop(0, lats - 1, gather_sums, 0)

    forward_sums()
    halves = []
    for slot in (1, 0, 2):
        halo_arrived(back_halo, slot)
        fill_windows(be, slot, True)
        block = taps(slot, True)
        halves.append(
            (
                matmul(windows[:, block], wcol_hi[block, :], ((1,), (0,))),
                matmul(windows[0:cols, block], wcol_lo[block, :], ((1,), (0,))),
            )
        )
    both = halves[0][0] + halves[1][0] + halves[2][0]
    small = halves[0][1] + halves[1][1] + halves[2][1]
    grad = (both[:cols] + both[cols:] + small).T
    igrad[...] = cot[...] + grad.reshape(lons, 8, cols)

    exchanged(shape_send, shaped, 3)
    out[...] = field[...] + shaped[...]

    await_bytes(fgbuf.at[pl.ds(0, lats - 1)], fa_recv)
    fgbuf[sum_slot] = fgpart[...]
    for i in range(lons):
        fgrad[:, i] = fgbuf[i % lats, i // lats]

    for copy in field_halo + back_halo:
        copy.wait_send()
    for h in range(groups):
        @pl.when(share_of(a) + lats * h != d)
        def _():
            await_bytes(gpart.at[h], gp_send.at[h])

        @pl.when(owners[h] != d)
        def _():
            await_bytes(fsum.at[h], fp_send.at[h])

    await_bytes(gbuf.at[pl.ds(0, lats - 1)], ga_send)
    await_bytes(rsbuf.at[0, pl.ds(0, lats - 1)], rs_send.at[0])

    @pl.when(own_share > 0)
    def _():
        await_bytes(pbuf.at[lats], rs_send.at[1])

    await_bytes(fgbuf.at[pl.ds(0, lats - 1)], fa_send)
    for index, src in enumerate((cot, mixed, back_send, shape_send)):
        exchange_sent(src, index)


def store_kernel(*refs):
    sources, results, sems = refs[:3], refs[3:6], refs[6]
    copies = [
        pltpu.make_async_copy(src, dst, sems.at[i])
        for i, (src, dst) in enumerate(zip(sources, results))
    ]
    for copy in copies:
        copy.start()
    for copy in copies:
        copy.wait()


def solution(mesh):
    lats, lons = mesh.shape["lat"], mesh.shape["lon"]
    groups = lons // lats

    def on_device(field, cotangent, conv_weight, spectral_filter):
        chans, _, cols = field.shape
        residues, mats, twiddle = tables(lats, lons, cols)
        tiles = (lons, 8, cols)
        tile = jax.ShapeDtypeStruct(tiles, f32)
        vmem = pl.BlockSpec(memory_space=pltpu.VMEM)
        line = pltpu.VMEM(tiles, f32)
        dma = pltpu.SemaphoreType.DMA
        share = (groups, 2, 8, cols)
        shares = (lats,) + share
        out, igrad, fgrad = pl.pallas_call(
            functools.partial(layer_kernel, lats, lons, residues),
            out_shape=(tile, tile, jax.ShapeDtypeStruct((2,) + tiles, f32)),
            in_specs=[pl.BlockSpec(memory_space=pltpu.HBM)] * 6,
            out_specs=(vmem, vmem, vmem),
            scratch_shapes=[
                line, line,
                pltpu.VMEM((2,) + tiles, f32),
                pltpu.VMEM(mats.shape, bf16),
                pltpu.VMEM(twiddle.shape, f32),
                pltpu.VMEM((9, chans, chans), f32),
                pltpu.VMEM((chans, 9 * chans), bf16),
                pltpu.VMEM((chans, 9 * chans), bf16),
                pltpu.VMEM((9 * chans, chans), bf16),
                pltpu.VMEM((9 * chans, chans), bf16),
                pltpu.VMEM((3, cols + 16, chans), f32),
                pltpu.VMEM((3, cols + 16, chans), f32),
                pltpu.VMEM((2 * cols, 9 * chans), bf16),
                line, line, line, line, line, line, line,
                pltpu.VMEM((chans, 2 * cols), f32),
                pltpu.VMEM((2, chans, cols), f32),
                pltpu.VMEM(share, f32),
                pltpu.VMEM(shares, f32),
                pltpu.VMEM((lats + 1, 2, 8, cols), f32),
                pltpu.VMEM((2, lats, 2, 8, cols), f32),
                pltpu.VMEM(share, f32),
                pltpu.VMEM(share, f32),
                pltpu.VMEM(shares, f32),
                dma((6,)), dma((2, 8)), dma((2, 8)), dma((4,)), dma((4,)),
                dma((groups,)), dma((groups,)), dma, dma, dma((2,)), dma((2,)),
                dma((groups,)), dma((groups,)), dma, dma,
            ],
            compiler_params=pltpu.CompilerParams(
                collective_id=0, has_side_effects=True, vmem_limit_bytes=40 << 20
            ),
        )(
            *(
                pltpu.with_memory_space_constraint(v, pltpu.HBM)
                for v in (
                    field.reshape(tiles),
                    cotangent.reshape(tiles),
                    conv_weight.reshape(9, chans, chans),
                    spectral_filter.reshape((2,) + tiles),
                    jnp.asarray(mats),
                    jnp.asarray(twiddle),
                )
            )
        )
        anywhere = pl.BlockSpec(memory_space=pl.ANY)
        out, igrad, fgrad = pl.pallas_call(
            store_kernel,
            out_shape=tuple(jax.ShapeDtypeStruct(v.shape, f32) for v in (out, igrad, fgrad)),
            in_specs=[vmem] * 3,
            out_specs=(anywhere,) * 3,
            scratch_shapes=[dma((3,))],
            compiler_params=pltpu.CompilerParams(has_side_effects=True),
        )(*(pltpu.with_memory_space_constraint(v, pltpu.VMEM) for v in (out, igrad, fgrad)))
        shape = (chans, 1, cols)
        return out.reshape(shape), igrad.reshape(shape), fgrad.reshape(2, chans, cols)

    placed = (P(None, "lat", "lon"), P(None, "lat", "lon"), P(), P(None, None, "lon"))
    return jax.shard_map(
        on_device,
        mesh=mesh,
        in_specs=placed,
        out_specs=(P(None, "lat", "lon"), P(None, "lat", "lon"), P(None, None, "lon")),
        check_vma=False,
    )
```

```python
import functools
import math

import jax
import jax.numpy as jnp
import ml_dtypes
import numpy as np
from jax import lax
from jax.experimental import pallas as pl
from jax.experimental.pallas import tpu as pltpu
from jax.sharding import PartitionSpec as P

MESH = pl.DeviceIdType.MESH
f32, bf16 = jnp.float32, jnp.bfloat16


def split(value):
    high = value.astype(bf16)
    return high, (value - high.astype(f32)).astype(bf16)


def matmul(lhs, rhs, dims):
    return lax.dot_general(lhs, rhs, (dims, ((), ())), preferred_element_type=f32)


def turn(value, angle):
    re, im = value
    c, s = math.cos(angle), math.sin(angle)
    return re * c - im * s, im * c + re * s


def conj(value):
    return value[0], None if value[1] is None else -value[1]


def plus(a, b):
    if a[1] is None or b[1] is None:
        return a[0] + b[0], a[1] if b[1] is None else b[1]
    return a[0] + b[0], a[1] + b[1]


def minus(a, b):
    if a[1] is None or b[1] is None:
        return a[0] - b[0], a[1] if b[1] is None else -b[1]
    return a[0] - b[0], a[1] - b[1]


def real_forward(xs):
    n = len(xs)
    if n == 1:
        return [(xs[0], None)]
    if n == 2:
        return [(xs[0] + xs[1], None), (xs[0] - xs[1], None)]
    even, odd = real_forward(xs[0::2]), real_forward(xs[1::2])
    out = [None] * (n // 2 + 1)
    for r in range(n // 4 + 1):
        e, o = even[r], odd[r]
        if r == 0:
            out[0], out[n // 2] = (e[0] + o[0], None), (e[0] - o[0], None)
        elif r == n // 4:
            out[r] = (e[0], -o[0])
        else:
            o = turn(o, -2 * math.pi * r / n)
            out[r], out[n // 2 - r] = plus(e, o), conj(minus(e, o))
    return out


def real_inverse(spec):
    n = 2 * (len(spec) - 1)
    if n == 2:
        a, b = spec[0][0], spec[1][0]
        return [a + b, a - b]
    even, odd = [None] * (n // 4 + 1), [None] * (n // 4 + 1)
    for r in range(n // 4 + 1):
        a, b = spec[r], spec[n // 2 - r]
        if r == 0:
            even[0], odd[0] = (a[0] + b[0], None), (a[0] - b[0], None)
        elif r == n // 4:
            even[r], odd[r] = (2.0 * a[0], None), (-2.0 * a[1], None)
        else:
            b = conj(b)
            even[r], odd[r] = plus(a, b), turn(minus(a, b), 2 * math.pi * r / n)
    out = [None] * n
    out[0::2], out[1::2] = real_inverse(even), real_inverse(odd)
    return out


def flipped_bits(place, extent):
    width = extent.bit_length() - 1
    return sum((place >> bit & 1) << (width - 1 - bit) for bit in range(width))


def tables(lats, lons, columns):
    groups = lons // lats
    residues = [flipped_bits(slot % groups * lats + slot // groups, lons) for slot in range(lons)]
    m = np.arange(columns)
    inner = 2 * np.pi * (np.outer(m, m) % columns) / columns
    c, s = np.cos(inner), np.sin(inner)
    forward = np.block([[c, -s], [s, c]])
    inverse = np.block([[c, s], [-s, c]]) / (columns * lons)
    mats = []
    for mat in (forward, inverse):
        high = mat.astype(np.float32).astype(ml_dtypes.bfloat16)
        mats += [high, (mat - high.astype(np.float64)).astype(ml_dtypes.bfloat16)]
    outer = 2 * np.pi * np.outer(residues, m) / (columns * lons)
    twiddle = np.stack([np.cos(outer), np.sin(outer)]).astype(np.float32)
    return residues, np.stack(mats), twiddle


def layer_kernel(
    lats, lons, residues,
    field_in, cot_in, weight_in, gain_in, mats_in, twiddle_in,
    out, igrad, fgrad,
    field, cot, gain, mats, twiddle, wbuf, wrow_hi, wrow_lo, wcol_hi, wcol_lo, xe, be, windows,
    mixed, cot_line, mix_line, back_send, shape_send, back, shaped,
    lhs, cspec, gpart, gbuf, pbuf, rsbuf, fsum, fgpart, fgbuf,
    load_sem, halo_send, halo_recv, a2a_send, a2a_recv,
    gp_send, gp_recv, ga_send, ga_recv, rs_send, rs_recv, fp_send, fp_recv, fa_send, fa_recv,
):
    a, d = lax.axis_index("lat"), lax.axis_index("lon")
    groups = lons // lats
    cols = field.shape[2]
    chans = lons * 8
    ring = lons // 2

    def far_first(u):
        away = ring // 2 - (u + 2) // 4
        away = jnp.where(lax.rem((u + 2) // 2, 2) == 1, ring - away, away)
        half = lax.rem(d // ring + 1 - lax.rem(u, 2), 2)
        return half * ring + lax.rem(d + away, ring)
    up, down = lax.rem(a + 1, lats), lax.rem(a + lats - 1, lats)
    east, west = lax.rem(d + 1, lons), lax.rem(d + lons - 1, lons)

    def far_lat(v):
        ys = lats // 4
        u = v // 4
        y = jnp.where(u == 0, 2, jnp.where(u == 1, 1, jnp.where(u == 2, 3, 0)))
        x = lax.rem(a // (2 * ys) + 1 - lax.rem(v // 2, 2), 2)
        y = lax.rem(lax.rem(a // 2, ys) + y, ys)
        return (x * ys + y) * 2 + lax.rem(a + 1 - lax.rem(v, 2), 2)

    barrier = pltpu.get_barrier_semaphore()

    def greet(lat, lon):
        pl.semaphore_signal(barrier, inc=1, device_id=(lat, lon), device_id_type=MESH)

    def greet_lat(i, carry):
        greet(lax.rem(a + i, lats), d)
        return carry

    def greet_lon(i, carry):
        greet(a, far_first(i))
        return carry

    lax.fori_loop(0, lons - 1, greet_lon, 0)
    lax.fori_loop(1, lats, greet_lat, 0)
    for lat in (up, down):
        for lon in (east, west):
            greet(lat, lon)

    loads = [
        pltpu.make_async_copy(src, dst, load_sem.at[i])
        for i, (src, dst) in enumerate(
            [(field_in, field), (cot_in, cot), (gain_in, gain), (weight_in, wbuf), (twiddle_in, twiddle), (mats_in, mats)]
        )
    ]
    for load in loads:
        load.start()

    def send(src, dst, send_sem, recv_sem, lat, lon):
        copy = pltpu.make_async_remote_copy(
            src_ref=src, dst_ref=dst, send_sem=send_sem, recv_sem=recv_sem,
            device_id=(lat, lon), device_id_type=MESH,
        )
        copy.start()

    def await_bytes(ref, sem):
        pltpu.make_async_copy(ref, ref, sem).wait()

    def share_of(row):
        return lax.rem(row + lats - lax.rem(d, lats), lats)

    def exchange(src, dst, index):
        def step(i, carry):
            peer = far_first(i)
            send(src.at[peer], dst.at[d], a2a_send.at[index], a2a_recv.at[index], a, peer)
            return carry

        lax.fori_loop(0, lons - 1, step, 0)

    def exchanged(src, dst, index):
        await_bytes(dst.at[pl.ds(0, lons - 1)], a2a_recv.at[index])
        dst[d] = src[d]

    def exchange_sent(src, index):
        await_bytes(src.at[pl.ds(0, lons - 1)], a2a_send.at[index])

    low, high = pl.ds(0, 8), pl.ds(cols + 8, 8)
    middle = pl.ds(8, cols)
    rows = [(up, 0), (down, 2)]
    edges = [(up, 0), (a, 1), (down, 2)]

    def halo_plan(ext, index):
        plan = []
        for lat, slot in rows:
            plan.append((ext.at[1, middle], ext.at[slot, middle], lat, d))
        for lat, slot in edges:
            plan.append((ext.at[1, pl.ds(8, 8)], ext.at[slot, high], lat, west))
            plan.append((ext.at[1, pl.ds(cols, 8)], ext.at[slot, low], lat, east))
        return [
            pltpu.make_async_remote_copy(
                src_ref=src, dst_ref=dst, send_sem=halo_send.at[index, i],
                recv_sem=halo_recv.at[index, i], device_id=(lat, lon), device_id_type=MESH,
            )
            for i, (src, dst, lat, lon) in enumerate(plan)
        ]

    loads[0].wait()
    xe[1, middle] = field[...].reshape(chans, cols).T
    loads[1].wait()
    loads[2].wait()

    pl.semaphore_wait(barrier, lats - 1 + lons - 1 + 4)

    for h in range(groups):
        e = share_of(a) + lats * h

        @pl.when(e != d)
        def _():
            send(gain.at[:, e], gpart.at[d // lats], gp_send.at[h], gp_recv.at[d // lats], a, e)

        @pl.when(e == d)
        def _():
            gpart[d // lats] = gain[:, e]

    field_halo = halo_plan(xe, 0)
    for copy in field_halo:
        copy.start()

    exchange(cot, cot_line, 0)

    loads[3].wait()
    for t in range(9):
        w_hi, w_lo = split(wbuf[t])
        block = slice(t * chans, (t + 1) * chans)
        wrow_hi[:, block] = w_hi
        wrow_lo[:, block] = w_lo
        wcol_hi[block, :] = w_hi
        wcol_lo[block, :] = w_lo

    def fill_windows(ext, slot, backward):
        for s in range(3):
            t = (2 - slot if backward else slot) * 3 + s
            start = 9 - s if backward else 7 + s
            window = ext[slot, start : start + cols, :]
            if slot == 0:
                window = jnp.where(a > 0, window, 0.0)
            if slot == 2:
                window = jnp.where(a < lats - 1, window, 0.0)
            w_hi, w_lo = split(window)
            block = slice(t * chans, (t + 1) * chans)
            windows[0:cols, block] = w_hi
            windows[cols : 2 * cols, block] = w_lo

    def halo_arrived(plan, slot):
        for i in {0: (0, 2, 3), 1: (4, 5), 2: (1, 6, 7)}[slot]:
            plan[i].wait_recv()

    def taps(slot, backward):
        first = 2 - slot if backward else slot
        return slice(first * 3 * chans, (first * 3 + 3) * chans)

    gain_slot = share_of(a)
    own_share = share_of(a)

    def forward_gain():
        for i in range(groups):
            g = lax.rem(d // lats + i, groups)

            @pl.when(gain_slot + lats * g != d)
            def _():
                await_bytes(gpart.at[g], gp_recv.at[g])

            def gather_gain(i, carry):
                send(gpart.at[g], gbuf.at[gain_slot, g], ga_send, ga_recv, far_lat(i), d)
                return carry

            lax.fori_loop(0, lats - 1, gather_gain, 0)

    halves = []
    for slot in (1, 0, 2):
        halo_arrived(field_halo, slot)
        fill_windows(xe, slot, False)
        block = taps(slot, False)
        halves.append(
            (
                matmul(wrow_hi[:, block], windows[:, block], ((1,), (1,))),
                matmul(wrow_lo[:, block], windows[0:cols, block], ((1,), (1,))),
            )
        )
    both = halves[0][0] + halves[1][0] + halves[2][0]
    small = halves[0][1] + halves[1][1] + halves[2][1]
    mixed[...] = (both[:, :cols] + both[:, cols:] + small).reshape(lons, 8, cols)
    exchange(mixed, mix_line, 1)
    forward_gain()

    def transform(line):
        spec = real_forward([line[i] for i in range(lons)])
        for slot, r in enumerate(residues):
            re, im = spec[r] if 2 * r <= lons else conj(spec[lons - r])
            c, s = twiddle[0, slot : slot + 1, :], twiddle[1, slot : slot + 1, :]
            block = slice(slot * 8, slot * 8 + 8)
            if im is None:
                lhs[block, 0:cols] = re * c
                lhs[block, cols : 2 * cols] = -re * s
            else:
                lhs[block, 0:cols] = re * c + im * s
                lhs[block, cols : 2 * cols] = im * c - re * s
        hi, lo = split(lhs[...])
        dims = ((1,), (0,))
        full = matmul(hi, mats[0], dims) + matmul(hi, mats[1], dims) + matmul(lo, mats[0], dims)
        return full[:, :cols], full[:, cols:]

    def untransform(re, im, dst):
        hi, lo = split(jnp.concatenate([re, im], axis=1))
        dims = ((1,), (0,))
        lhs[...] = matmul(hi, mats[2], dims) + matmul(hi, mats[3], dims) + matmul(lo, mats[2], dims)
        turned = [None] * lons
        for slot, r in enumerate(residues):
            block = slice(slot * 8, slot * 8 + 8)
            c, s = twiddle[0, slot : slot + 1, :], twiddle[1, slot : slot + 1, :]
            re, im = lhs[block, 0:cols], lhs[block, cols : 2 * cols]
            turned[r] = (re * c - im * s, im * c + re * s)
        half = [(turned[0][0], None)]
        for r in range(1, lons // 2):
            half.append(tuple(0.5 * v for v in plus(turned[r], conj(turned[lons - r]))))
        half.append((turned[lons // 2][0], None))
        for i, value in enumerate(real_inverse(half)):
            dst[i] = value

    loads[4].wait()
    loads[5].wait()
    exchanged(cot, cot_line, 0)
    c_re, c_im = transform(cot_line)
    cspec[0] = c_re
    cspec[1] = c_im
    await_bytes(gbuf.at[pl.ds(0, lats - 1)], ga_recv)
    gbuf[gain_slot] = gpart[...]
    g_re = gbuf[:, :, 0].reshape(chans, cols)
    g_im = gbuf[:, :, 1].reshape(chans, cols)
    untransform(g_re * c_re + g_im * c_im, g_re * c_im - g_im * c_re, back_send)
    exchange(back_send, back, 2)

    exchanged(mixed, mix_line, 1)
    s_re, s_im = transform(mix_line)
    c_re, c_im = cspec[0], cspec[1]
    scale = 1.0 / (cols * lons)
    for slot, r in enumerate(residues):
        if r <= lats:
            block = slice(slot * 8, slot * 8 + 8)
            pbuf[r, 0] = (s_re[block] * c_re[block] + s_im[block] * c_im[block]) * scale
            pbuf[r, 1] = (s_re[block] * c_im[block] - s_im[block] * c_re[block]) * scale

    def scatter_sums(i, carry):
        peer = far_lat(i)
        share = share_of(peer)
        send(pbuf.at[share], rsbuf.at[0, a], rs_send.at[0], rs_recv.at[0], peer, d)

        @pl.when(share == 0)
        def _():
            send(pbuf.at[lats], rsbuf.at[1, a], rs_send.at[1], rs_recv.at[1], peer, d)

        return carry

    lax.fori_loop(0, lats - 1, scatter_sums, 0)

    g_re = gbuf[:, :, 0].reshape(chans, cols)
    g_im = gbuf[:, :, 1].reshape(chans, cols)
    untransform(g_re * s_re - g_im * s_im, g_re * s_im + g_im * s_re, shape_send)

    await_bytes(rsbuf.at[0, pl.ds(0, lats - 1)], rs_recv.at[0])
    rsbuf[0, a] = pbuf[own_share]
    fsum[0] = jnp.sum(rsbuf[0], axis=0)

    @pl.when(own_share == 0)
    def _():
        await_bytes(rsbuf.at[1, pl.ds(0, lats - 1)], rs_recv.at[1])
        rsbuf[1, a] = pbuf[lats]
        fsum[1] = jnp.sum(rsbuf[1], axis=0)

    @pl.when(own_share > 0)
    def _():
        value = fsum[0].reshape(16, cols)
        first, rest = split(value)
        second, third = split(value - first.astype(f32) - rest.astype(f32))
        place = lax.broadcasted_iota(jnp.int32, (cols, cols), 0)
        other = lax.broadcasted_iota(jnp.int32, (cols, cols), 1)
        mirror = jnp.where(place + other == cols - 1, 1.0, 0.0).astype(bf16)
        parts = [matmul(part, mirror, ((1,), (0,))) for part in (first, rest, second)]
        value = (parts[0] + parts[1] + parts[2]).reshape(2, 8, cols)
        fsum[1, 0] = value[0]
        fsum[1, 1] = -value[1]

    def owner_of(residue):
        width = lons.bit_length() - 1
        return sum(lax.rem(residue // 2**bit, 2) * 2 ** (width - 1 - bit) for bit in range(width))

    owners = [owner_of(own_share), owner_of(jnp.where(own_share == 0, lats, lons - own_share))]
    for h, e in enumerate(owners):
        @pl.when(e != d)
        def _():
            send(fsum.at[h], fgpart.at[d // lats], fp_send.at[h], fp_recv.at[d // lats], a, e)

        @pl.when(e == d)
        def _():
            fgpart[d // lats] = fsum[h]

    exchanged(back_send, back, 2)
    be[1, middle] = back[...].reshape(chans, cols).T
    back_halo = halo_plan(be, 1)
    for copy in back_halo:
        copy.start()

    residue = owner_of(d)
    group = jnp.where(residue < lats, residue, lax.rem(lons - residue, lats))
    sum_slot = lax.rem(a + lats - group, lats)

    def forward_sums():
        for i in range(groups):
            g = lax.rem(d // lats + i, groups)

            @pl.when(sum_slot + lats * g != d)
            def _():
                await_bytes(fgpart.at[g], fp_recv.at[g])

            def gather_sums(i, carry):
                send(fgpart.at[g], fgbuf.at[sum_slot, g], fa_send, fa_recv, far_lat(i), d)
                return carry

            lax.fori_loop(0, lats - 1, gather_sums, 0)

    exchange(shape_send, shaped, 3)
    forward_sums()
    halves = []
    for slot in (1, 0, 2):
        halo_arrived(back_halo, slot)
        fill_windows(be, slot, True)
        block = taps(slot, True)
        halves.append(
            (
                matmul(windows[:, block], wcol_hi[block, :], ((1,), (0,))),
                matmul(windows[0:cols, block], wcol_lo[block, :], ((1,), (0,))),
            )
        )
    both = halves[0][0] + halves[1][0] + halves[2][0]
    small = halves[0][1] + halves[1][1] + halves[2][1]
    grad = (both[:cols] + both[cols:] + small).T
    igrad[...] = cot[...] + grad.reshape(lons, 8, cols)

    exchanged(shape_send, shaped, 3)
    out[...] = field[...] + shaped[...]

    await_bytes(fgbuf.at[pl.ds(0, lats - 1)], fa_recv)
    fgbuf[sum_slot] = fgpart[...]
    for i in range(lons):
        fgrad[:, i] = fgbuf[i % lats, i // lats]

    for copy in field_halo + back_halo:
        copy.wait_send()
    for h in range(groups):
        @pl.when(share_of(a) + lats * h != d)
        def _():
            await_bytes(gpart.at[h], gp_send.at[h])

        @pl.when(owners[h] != d)
        def _():
            await_bytes(fsum.at[h], fp_send.at[h])

    await_bytes(gbuf.at[pl.ds(0, lats - 1)], ga_send)
    await_bytes(rsbuf.at[0, pl.ds(0, lats - 1)], rs_send.at[0])

    @pl.when(own_share > 0)
    def _():
        await_bytes(pbuf.at[lats], rs_send.at[1])

    await_bytes(fgbuf.at[pl.ds(0, lats - 1)], fa_send)
    for index, src in enumerate((cot, mixed, back_send, shape_send)):
        exchange_sent(src, index)


def store_kernel(*refs):
    sources, results, sems = refs[:3], refs[3:6], refs[6]
    copies = [
        pltpu.make_async_copy(src, dst, sems.at[i])
        for i, (src, dst) in enumerate(zip(sources, results))
    ]
    for copy in copies:
        copy.start()
    for copy in copies:
        copy.wait()


def solution(mesh):
    lats, lons = mesh.shape["lat"], mesh.shape["lon"]
    groups = lons // lats

    def on_device(field, cotangent, conv_weight, spectral_filter):
        chans, _, cols = field.shape
        residues, mats, twiddle = tables(lats, lons, cols)
        tiles = (lons, 8, cols)
        tile = jax.ShapeDtypeStruct(tiles, f32)
        vmem = pl.BlockSpec(memory_space=pltpu.VMEM)
        line = pltpu.VMEM(tiles, f32)
        dma = pltpu.SemaphoreType.DMA
        share = (groups, 2, 8, cols)
        shares = (lats,) + share
        out, igrad, fgrad = pl.pallas_call(
            functools.partial(layer_kernel, lats, lons, residues),
            out_shape=(tile, tile, jax.ShapeDtypeStruct((2,) + tiles, f32)),
            in_specs=[pl.BlockSpec(memory_space=pltpu.HBM)] * 6,
            out_specs=(vmem, vmem, vmem),
            scratch_shapes=[
                line, line,
                pltpu.VMEM((2,) + tiles, f32),
                pltpu.VMEM(mats.shape, bf16),
                pltpu.VMEM(twiddle.shape, f32),
                pltpu.VMEM((9, chans, chans), f32),
                pltpu.VMEM((chans, 9 * chans), bf16),
                pltpu.VMEM((chans, 9 * chans), bf16),
                pltpu.VMEM((9 * chans, chans), bf16),
                pltpu.VMEM((9 * chans, chans), bf16),
                pltpu.VMEM((3, cols + 16, chans), f32),
                pltpu.VMEM((3, cols + 16, chans), f32),
                pltpu.VMEM((2 * cols, 9 * chans), bf16),
                line, line, line, line, line, line, line,
                pltpu.VMEM((chans, 2 * cols), f32),
                pltpu.VMEM((2, chans, cols), f32),
                pltpu.VMEM(share, f32),
                pltpu.VMEM(shares, f32),
                pltpu.VMEM((lats + 1, 2, 8, cols), f32),
                pltpu.VMEM((2, lats, 2, 8, cols), f32),
                pltpu.VMEM(share, f32),
                pltpu.VMEM(share, f32),
                pltpu.VMEM(shares, f32),
                dma((6,)), dma((2, 8)), dma((2, 8)), dma((4,)), dma((4,)),
                dma((groups,)), dma((groups,)), dma, dma, dma((2,)), dma((2,)),
                dma((groups,)), dma((groups,)), dma, dma,
            ],
            compiler_params=pltpu.CompilerParams(
                collective_id=0, has_side_effects=True, vmem_limit_bytes=40 << 20
            ),
        )(
            *(
                pltpu.with_memory_space_constraint(v, pltpu.HBM)
                for v in (
                    field.reshape(tiles),
                    cotangent.reshape(tiles),
                    conv_weight.reshape(9, chans, chans),
                    spectral_filter.reshape((2,) + tiles),
                    jnp.asarray(mats),
                    jnp.asarray(twiddle),
                )
            )
        )
        anywhere = pl.BlockSpec(memory_space=pl.ANY)
        out, igrad, fgrad = pl.pallas_call(
            store_kernel,
            out_shape=tuple(jax.ShapeDtypeStruct(v.shape, f32) for v in (out, igrad, fgrad)),
            in_specs=[vmem] * 3,
            out_specs=(anywhere,) * 3,
            scratch_shapes=[dma((3,))],
            compiler_params=pltpu.CompilerParams(has_side_effects=True),
        )(*(pltpu.with_memory_space_constraint(v, pltpu.VMEM) for v in (out, igrad, fgrad)))
        shape = (chans, 1, cols)
        return out.reshape(shape), igrad.reshape(shape), fgrad.reshape(2, chans, cols)

    placed = (P(None, "lat", "lon"), P(None, "lat", "lon"), P(), P(None, None, "lon"))
    return jax.shard_map(
        on_device,
        mesh=mesh,
        in_specs=placed,
        out_specs=(P(None, "lat", "lon"), P(None, "lat", "lon"), P(None, None, "lon")),
        check_vma=False,
    )
```

```python
import functools
import math

import jax
import jax.numpy as jnp
import ml_dtypes
import numpy as np
from jax import lax
from jax.experimental import pallas as pl
from jax.experimental.pallas import tpu as pltpu
from jax.sharding import PartitionSpec as P

MESH = pl.DeviceIdType.MESH
f32, bf16 = jnp.float32, jnp.bfloat16


def split(value):
    high = value.astype(bf16)
    return high, (value - high.astype(f32)).astype(bf16)


def matmul(lhs, rhs, dims):
    return lax.dot_general(lhs, rhs, (dims, ((), ())), preferred_element_type=f32)


def turn(value, angle):
    re, im = value
    c, s = math.cos(angle), math.sin(angle)
    return re * c - im * s, im * c + re * s


def conj(value):
    return value[0], None if value[1] is None else -value[1]


def plus(a, b):
    if a[1] is None or b[1] is None:
        return a[0] + b[0], a[1] if b[1] is None else b[1]
    return a[0] + b[0], a[1] + b[1]


def minus(a, b):
    if a[1] is None or b[1] is None:
        return a[0] - b[0], a[1] if b[1] is None else -b[1]
    return a[0] - b[0], a[1] - b[1]


def real_forward(xs):
    n = len(xs)
    if n == 1:
        return [(xs[0], None)]
    if n == 2:
        return [(xs[0] + xs[1], None), (xs[0] - xs[1], None)]
    even, odd = real_forward(xs[0::2]), real_forward(xs[1::2])
    out = [None] * (n // 2 + 1)
    for r in range(n // 4 + 1):
        e, o = even[r], odd[r]
        if r == 0:
            out[0], out[n // 2] = (e[0] + o[0], None), (e[0] - o[0], None)
        elif r == n // 4:
            out[r] = (e[0], -o[0])
        else:
            o = turn(o, -2 * math.pi * r / n)
            out[r], out[n // 2 - r] = plus(e, o), conj(minus(e, o))
    return out


def real_inverse(spec):
    n = 2 * (len(spec) - 1)
    if n == 2:
        a, b = spec[0][0], spec[1][0]
        return [a + b, a - b]
    even, odd = [None] * (n // 4 + 1), [None] * (n // 4 + 1)
    for r in range(n // 4 + 1):
        a, b = spec[r], spec[n // 2 - r]
        if r == 0:
            even[0], odd[0] = (a[0] + b[0], None), (a[0] - b[0], None)
        elif r == n // 4:
            even[r], odd[r] = (2.0 * a[0], None), (-2.0 * a[1], None)
        else:
            b = conj(b)
            even[r], odd[r] = plus(a, b), turn(minus(a, b), 2 * math.pi * r / n)
    out = [None] * n
    out[0::2], out[1::2] = real_inverse(even), real_inverse(odd)
    return out


def flipped_bits(place, extent):
    width = extent.bit_length() - 1
    return sum((place >> bit & 1) << (width - 1 - bit) for bit in range(width))


def tables(lats, lons, columns):
    groups = lons // lats
    residues = [flipped_bits(slot % groups * lats + slot // groups, lons) for slot in range(lons)]
    m = np.arange(columns)
    inner = 2 * np.pi * (np.outer(m, m) % columns) / columns
    c, s = np.cos(inner), np.sin(inner)
    forward = np.block([[c, -s], [s, c]])
    inverse = np.block([[c, s], [-s, c]]) / (columns * lons)
    mats = []
    for mat in (forward, inverse):
        high = mat.astype(np.float32).astype(ml_dtypes.bfloat16)
        low = (mat - high.astype(np.float64)).astype(ml_dtypes.bfloat16)
        mats.append(np.concatenate([high, low, high]))
    outer = 2 * np.pi * np.outer(residues, m) / (columns * lons)
    twiddle = np.stack([np.cos(outer), np.sin(outer)]).astype(np.float32)
    return residues, np.stack(mats), twiddle


def layer_kernel(
    lats, lons, residues,
    field_in, cot_in, weight_in, gain_in, mats_in, twiddle_in,
    out, igrad, fgrad,
    field, cot, gain, mats, twiddle, wbuf, wrow_hi, wrow_lo, wcol_hi, wcol_lo, xe, be, windows,
    mixed, cot_line, mix_line, back_send, shape_send, back, shaped,
    lhs, cspec, gpart, gbuf, pbuf, rsbuf, fsum, fgpart, fgbuf,
    load_sem, halo_send, halo_recv, a2a_send, a2a_recv,
    gp_send, gp_recv, ga_send, ga_recv, rs_send, rs_recv, fp_send, fp_recv, fa_send, fa_recv,
):
    a, d = lax.axis_index("lat"), lax.axis_index("lon")
    groups = lons // lats
    cols = field.shape[2]
    chans = lons * 8
    ring = lons // 2

    def far_first(u):
        away = ring // 2 - (u + 2) // 4
        away = jnp.where(lax.rem((u + 2) // 2, 2) == 1, ring - away, away)
        half = lax.rem(d // ring + 1 - lax.rem(u, 2), 2)
        return half * ring + lax.rem(d + away, ring)
    up, down = lax.rem(a + 1, lats), lax.rem(a + lats - 1, lats)
    east, west = lax.rem(d + 1, lons), lax.rem(d + lons - 1, lons)

    def far_lat(v):
        ys = lats // 4
        u = v // 4
        y = jnp.where(u == 0, 2, jnp.where(u == 1, 1, jnp.where(u == 2, 3, 0)))
        x = lax.rem(a // (2 * ys) + 1 - lax.rem(v // 2, 2), 2)
        y = lax.rem(lax.rem(a // 2, ys) + y, ys)
        return (x * ys + y) * 2 + lax.rem(a + 1 - lax.rem(v, 2), 2)

    barrier = pltpu.get_barrier_semaphore()

    def greet(lat, lon):
        pl.semaphore_signal(barrier, inc=1, device_id=(lat, lon), device_id_type=MESH)

    def greet_lat(i, carry):
        greet(lax.rem(a + i, lats), d)
        return carry

    def greet_lon(i, carry):
        greet(a, far_first(i))
        return carry

    lax.fori_loop(0, lons - 1, greet_lon, 0)
    lax.fori_loop(1, lats, greet_lat, 0)
    for lat in (up, down):
        for lon in (east, west):
            greet(lat, lon)

    loads = [
        pltpu.make_async_copy(src, dst, load_sem.at[i])
        for i, (src, dst) in enumerate(
            [(field_in, field), (cot_in, cot), (gain_in, gain), (weight_in, wbuf), (twiddle_in, twiddle), (mats_in, mats)]
        )
    ]
    for load in loads:
        load.start()

    def send(src, dst, send_sem, recv_sem, lat, lon):
        copy = pltpu.make_async_remote_copy(
            src_ref=src, dst_ref=dst, send_sem=send_sem, recv_sem=recv_sem,
            device_id=(lat, lon), device_id_type=MESH,
        )
        copy.start()

    def await_bytes(ref, sem):
        pltpu.make_async_copy(ref, ref, sem).wait()

    def share_of(row):
        return lax.rem(row + lats - lax.rem(d, lats), lats)

    def exchange(src, dst, index):
        def step(i, carry):
            peer = far_first(i)
            send(src.at[peer], dst.at[d], a2a_send.at[index], a2a_recv.at[index], a, peer)
            return carry

        lax.fori_loop(0, lons - 1, step, 0)

    def exchanged(src, dst, index):
        await_bytes(dst.at[pl.ds(0, lons - 1)], a2a_recv.at[index])
        dst[d] = src[d]

    def exchange_sent(src, index):
        await_bytes(src.at[pl.ds(0, lons - 1)], a2a_send.at[index])

    low, high = pl.ds(0, 8), pl.ds(cols + 8, 8)
    middle = pl.ds(8, cols)
    rows = [(up, 0), (down, 2)]
    edges = [(up, 0), (a, 1), (down, 2)]

    def halo_plan(ext, index):
        plan = []
        for lat, slot in rows:
            plan.append((ext.at[1, middle], ext.at[slot, middle], lat, d))
        for lat, slot in edges:
            plan.append((ext.at[1, pl.ds(8, 8)], ext.at[slot, high], lat, west))
            plan.append((ext.at[1, pl.ds(cols, 8)], ext.at[slot, low], lat, east))
        return [
            pltpu.make_async_remote_copy(
                src_ref=src, dst_ref=dst, send_sem=halo_send.at[index, i],
                recv_sem=halo_recv.at[index, i], device_id=(lat, lon), device_id_type=MESH,
            )
            for i, (src, dst, lat, lon) in enumerate(plan)
        ]

    loads[0].wait()
    xe[1, middle] = field[...].reshape(chans, cols).T
    loads[1].wait()
    loads[2].wait()

    pl.semaphore_wait(barrier, lats - 1 + lons - 1 + 4)

    field_halo = halo_plan(xe, 0)
    for copy in field_halo:
        copy.start()

    for h in range(groups):
        e = share_of(a) + lats * h

        @pl.when(e != d)
        def _():
            send(gain.at[:, e], gpart.at[d // lats], gp_send.at[h], gp_recv.at[d // lats], a, e)

        @pl.when(e == d)
        def _():
            gpart[d // lats] = gain[:, e]

    exchange(cot, cot_line, 0)

    loads[3].wait()
    for t in range(9):
        w_hi, w_lo = split(wbuf[t])
        block = slice(t * chans, (t + 1) * chans)
        wrow_hi[:, block] = w_hi
        wrow_lo[:, block] = w_lo
        wcol_hi[block, :] = w_hi
        wcol_lo[block, :] = w_lo

    def fill_windows(ext, slot, backward):
        for s in range(3):
            t = (2 - slot if backward else slot) * 3 + s
            start = 9 - s if backward else 7 + s
            window = ext[slot, start : start + cols, :]
            if slot == 0:
                window = jnp.where(a > 0, window, 0.0)
            if slot == 2:
                window = jnp.where(a < lats - 1, window, 0.0)
            w_hi, w_lo = split(window)
            block = slice(t * chans, (t + 1) * chans)
            windows[0:cols, block] = w_hi
            windows[cols : 2 * cols, block] = w_lo

    def halo_arrived(plan, slot):
        for i in {0: (0, 2, 3), 1: (4, 5), 2: (1, 6, 7)}[slot]:
            plan[i].wait_recv()

    def taps(slot, backward):
        first = 2 - slot if backward else slot
        return slice(first * 3 * chans, (first * 3 + 3) * chans)

    gain_slot = share_of(a)
    own_share = share_of(a)

    def forward_gain():
        for i in range(groups):
            g = lax.rem(d // lats + i, groups)

            @pl.when(gain_slot + lats * g != d)
            def _():
                await_bytes(gpart.at[g], gp_recv.at[g])

            def gather_gain(i, carry):
                send(gpart.at[g], gbuf.at[gain_slot, g], ga_send, ga_recv, far_lat(i), d)
                return carry

            lax.fori_loop(0, lats - 1, gather_gain, 0)

    halves = []
    for slot in (1, 0, 2):
        halo_arrived(field_halo, slot)
        fill_windows(xe, slot, False)
        block = taps(slot, False)
        halves.append(
            (
                matmul(wrow_hi[:, block], windows[:, block], ((1,), (1,))),
                matmul(wrow_lo[:, block], windows[0:cols, block], ((1,), (1,))),
            )
        )
    both = halves[0][0] + halves[1][0] + halves[2][0]
    small = halves[0][1] + halves[1][1] + halves[2][1]
    mixed[...] = (both[:, :cols] + both[:, cols:] + small).reshape(lons, 8, cols)
    exchange(mixed, mix_line, 1)
    forward_gain()

    def transform(line):
        spec = real_forward([line[i] for i in range(lons)])
        for slot, r in enumerate(residues):
            re, im = spec[r] if 2 * r <= lons else conj(spec[lons - r])
            c, s = twiddle[0, slot : slot + 1, :], twiddle[1, slot : slot + 1, :]
            block = slice(slot * 8, slot * 8 + 8)
            if im is None:
                lhs[block, 0:cols] = re * c
                lhs[block, cols : 2 * cols] = -re * s
            else:
                lhs[block, 0:cols] = re * c + im * s
                lhs[block, cols : 2 * cols] = im * c - re * s
        hi, lo = split(lhs[...])
        full = matmul(jnp.concatenate([hi, hi, lo], axis=1), mats[0], ((1,), (0,)))
        return full[:, :cols], full[:, cols:]

    def untransform(re, im, dst):
        hi, lo = split(jnp.concatenate([re, im], axis=1))
        lhs[...] = matmul(jnp.concatenate([hi, hi, lo], axis=1), mats[1], ((1,), (0,)))
        turned = [None] * lons
        for slot, r in enumerate(residues):
            block = slice(slot * 8, slot * 8 + 8)
            c, s = twiddle[0, slot : slot + 1, :], twiddle[1, slot : slot + 1, :]
            re, im = lhs[block, 0:cols], lhs[block, cols : 2 * cols]
            turned[r] = (re * c - im * s, im * c + re * s)
        half = [(turned[0][0], None)]
        for r in range(1, lons // 2):
            half.append(tuple(0.5 * v for v in plus(turned[r], conj(turned[lons - r]))))
        half.append((turned[lons // 2][0], None))
        for i, value in enumerate(real_inverse(half)):
            dst[i] = value

    loads[4].wait()
    loads[5].wait()
    exchanged(cot, cot_line, 0)
    c_re, c_im = transform(cot_line)
    cspec[0] = c_re
    cspec[1] = c_im
    await_bytes(gbuf.at[pl.ds(0, lats - 1)], ga_recv)
    gbuf[gain_slot] = gpart[...]
    g_re = gbuf[:, :, 0].reshape(chans, cols)
    g_im = gbuf[:, :, 1].reshape(chans, cols)
    untransform(g_re * c_re + g_im * c_im, g_re * c_im - g_im * c_re, back_send)
    exchange(back_send, back, 2)

    exchanged(mixed, mix_line, 1)
    s_re, s_im = transform(mix_line)
    c_re, c_im = cspec[0], cspec[1]
    scale = 1.0 / (cols * lons)
    for slot, r in enumerate(residues):
        if r <= lats:
            block = slice(slot * 8, slot * 8 + 8)
            pbuf[r, 0] = (s_re[block] * c_re[block] + s_im[block] * c_im[block]) * scale
            pbuf[r, 1] = (s_re[block] * c_im[block] - s_im[block] * c_re[block]) * scale

    def scatter_sums(i, carry):
        peer = far_lat(i)
        share = share_of(peer)
        send(pbuf.at[share], rsbuf.at[0, a], rs_send.at[0], rs_recv.at[0], peer, d)

        @pl.when(share == 0)
        def _():
            send(pbuf.at[lats], rsbuf.at[1, a], rs_send.at[1], rs_recv.at[1], peer, d)

        return carry

    lax.fori_loop(0, lats - 1, scatter_sums, 0)

    g_re = gbuf[:, :, 0].reshape(chans, cols)
    g_im = gbuf[:, :, 1].reshape(chans, cols)
    untransform(g_re * s_re - g_im * s_im, g_re * s_im + g_im * s_re, shape_send)

    await_bytes(rsbuf.at[0, pl.ds(0, lats - 1)], rs_recv.at[0])
    rsbuf[0, a] = pbuf[own_share]
    fsum[0] = jnp.sum(rsbuf[0], axis=0)

    def owner_of(residue):
        width = lons.bit_length() - 1
        return sum(lax.rem(residue // 2**bit, 2) * 2 ** (width - 1 - bit) for bit in range(width))

    owners = [owner_of(own_share), owner_of(jnp.where(own_share == 0, lats, lons - own_share))]
    def pass_on(h):
        e = owners[h]

        @pl.when(e != d)
        def _():
            send(fsum.at[h], fgpart.at[d // lats], fp_send.at[h], fp_recv.at[d // lats], a, e)

        @pl.when(e == d)
        def _():
            fgpart[d // lats] = fsum[h]

    pass_on(0)

    @pl.when(own_share == 0)
    def _():
        await_bytes(rsbuf.at[1, pl.ds(0, lats - 1)], rs_recv.at[1])
        rsbuf[1, a] = pbuf[lats]
        fsum[1] = jnp.sum(rsbuf[1], axis=0)

    @pl.when(own_share > 0)
    def _():
        value = fsum[0].reshape(16, cols)
        first, rest = split(value)
        second, third = split(value - first.astype(f32) - rest.astype(f32))
        place = lax.broadcasted_iota(jnp.int32, (cols, cols), 0)
        other = lax.broadcasted_iota(jnp.int32, (cols, cols), 1)
        mirror = jnp.where(place + other == cols - 1, 1.0, 0.0).astype(bf16)
        parts = [matmul(part, mirror, ((1,), (0,))) for part in (first, rest, second)]
        value = (parts[0] + parts[1] + parts[2]).reshape(2, 8, cols)
        fsum[1, 0] = value[0]
        fsum[1, 1] = -value[1]

    pass_on(1)

    exchanged(back_send, back, 2)
    be[1, middle] = back[...].reshape(chans, cols).T
    back_halo = halo_plan(be, 1)
    for copy in back_halo:
        copy.start()

    residue = owner_of(d)
    group = jnp.where(residue < lats, residue, lax.rem(lons - residue, lats))
    sum_slot = lax.rem(a + lats - group, lats)

    def forward_sums():
        for i in range(groups):
            g = lax.rem(d // lats + i, groups)

            @pl.when(sum_slot + lats * g != d)
            def _():
                await_bytes(fgpart.at[g], fp_recv.at[g])

            def gather_sums(i, carry):
                send(fgpart.at[g], fgbuf.at[sum_slot, g], fa_send, fa_recv, far_lat(i), d)
                return carry

            lax.fori_loop(0, lats - 1, gather_sums, 0)

    exchange(shape_send, shaped, 3)
    forward_sums()
    halves = []
    for slot in (1, 0, 2):
        halo_arrived(back_halo, slot)
        fill_windows(be, slot, True)
        block = taps(slot, True)
        halves.append(
            (
                matmul(windows[:, block], wcol_hi[block, :], ((1,), (0,))),
                matmul(windows[0:cols, block], wcol_lo[block, :], ((1,), (0,))),
            )
        )
    both = halves[0][0] + halves[1][0] + halves[2][0]
    small = halves[0][1] + halves[1][1] + halves[2][1]
    grad = (both[:cols] + both[cols:] + small).T
    igrad[...] = cot[...] + grad.reshape(lons, 8, cols)

    exchanged(shape_send, shaped, 3)
    out[...] = field[...] + shaped[...]

    await_bytes(fgbuf.at[pl.ds(0, lats - 1)], fa_recv)
    fgbuf[sum_slot] = fgpart[...]
    for i in range(lons):
        fgrad[:, i] = fgbuf[i % lats, i // lats]

    for copy in field_halo + back_halo:
        copy.wait_send()
    for h in range(groups):
        @pl.when(share_of(a) + lats * h != d)
        def _():
            await_bytes(gpart.at[h], gp_send.at[h])

        @pl.when(owners[h] != d)
        def _():
            await_bytes(fsum.at[h], fp_send.at[h])

    await_bytes(gbuf.at[pl.ds(0, lats - 1)], ga_send)
    await_bytes(rsbuf.at[0, pl.ds(0, lats - 1)], rs_send.at[0])

    @pl.when(own_share > 0)
    def _():
        await_bytes(pbuf.at[lats], rs_send.at[1])

    await_bytes(fgbuf.at[pl.ds(0, lats - 1)], fa_send)
    for index, src in enumerate((cot, mixed, back_send, shape_send)):
        exchange_sent(src, index)


def store_kernel(*refs):
    sources, results, sems = refs[:3], refs[3:6], refs[6]
    copies = [
        pltpu.make_async_copy(src, dst, sems.at[i])
        for i, (src, dst) in enumerate(zip(sources, results))
    ]
    for copy in copies:
        copy.start()
    for copy in copies:
        copy.wait()


def solution(mesh):
    lats, lons = mesh.shape["lat"], mesh.shape["lon"]
    groups = lons // lats

    def on_device(field, cotangent, conv_weight, spectral_filter):
        chans, _, cols = field.shape
        residues, mats, twiddle = tables(lats, lons, cols)
        tiles = (lons, 8, cols)
        tile = jax.ShapeDtypeStruct(tiles, f32)
        vmem = pl.BlockSpec(memory_space=pltpu.VMEM)
        line = pltpu.VMEM(tiles, f32)
        dma = pltpu.SemaphoreType.DMA
        share = (groups, 2, 8, cols)
        shares = (lats,) + share
        out, igrad, fgrad = pl.pallas_call(
            functools.partial(layer_kernel, lats, lons, residues),
            out_shape=(tile, tile, jax.ShapeDtypeStruct((2,) + tiles, f32)),
            in_specs=[pl.BlockSpec(memory_space=pltpu.HBM)] * 6,
            out_specs=(vmem, vmem, vmem),
            scratch_shapes=[
                line, line,
                pltpu.VMEM((2,) + tiles, f32),
                pltpu.VMEM(mats.shape, bf16),
                pltpu.VMEM(twiddle.shape, f32),
                pltpu.VMEM((9, chans, chans), f32),
                pltpu.VMEM((chans, 9 * chans), bf16),
                pltpu.VMEM((chans, 9 * chans), bf16),
                pltpu.VMEM((9 * chans, chans), bf16),
                pltpu.VMEM((9 * chans, chans), bf16),
                pltpu.VMEM((3, cols + 16, chans), f32),
                pltpu.VMEM((3, cols + 16, chans), f32),
                pltpu.VMEM((2 * cols, 9 * chans), bf16),
                line, line, line, line, line, line, line,
                pltpu.VMEM((chans, 2 * cols), f32),
                pltpu.VMEM((2, chans, cols), f32),
                pltpu.VMEM(share, f32),
                pltpu.VMEM(shares, f32),
                pltpu.VMEM((lats + 1, 2, 8, cols), f32),
                pltpu.VMEM((2, lats, 2, 8, cols), f32),
                pltpu.VMEM(share, f32),
                pltpu.VMEM(share, f32),
                pltpu.VMEM(shares, f32),
                dma((6,)), dma((2, 8)), dma((2, 8)), dma((4,)), dma((4,)),
                dma((groups,)), dma((groups,)), dma, dma, dma((2,)), dma((2,)),
                dma((groups,)), dma((groups,)), dma, dma,
            ],
            compiler_params=pltpu.CompilerParams(
                collective_id=0, has_side_effects=True, vmem_limit_bytes=40 << 20
            ),
        )(
            *(
                pltpu.with_memory_space_constraint(v, pltpu.HBM)
                for v in (
                    field.reshape(tiles),
                    cotangent.reshape(tiles),
                    conv_weight.reshape(9, chans, chans),
                    spectral_filter.reshape((2,) + tiles),
                    jnp.asarray(mats),
                    jnp.asarray(twiddle),
                )
            )
        )
        anywhere = pl.BlockSpec(memory_space=pl.ANY)
        out, igrad, fgrad = pl.pallas_call(
            store_kernel,
            out_shape=tuple(jax.ShapeDtypeStruct(v.shape, f32) for v in (out, igrad, fgrad)),
            in_specs=[vmem] * 3,
            out_specs=(anywhere,) * 3,
            scratch_shapes=[dma((3,))],
            compiler_params=pltpu.CompilerParams(has_side_effects=True),
        )(*(pltpu.with_memory_space_constraint(v, pltpu.VMEM) for v in (out, igrad, fgrad)))
        shape = (chans, 1, cols)
        return out.reshape(shape), igrad.reshape(shape), fgrad.reshape(2, chans, cols)

    placed = (P(None, "lat", "lon"), P(None, "lat", "lon"), P(), P(None, None, "lon"))
    return jax.shard_map(
        on_device,
        mesh=mesh,
        in_specs=placed,
        out_specs=(P(None, "lat", "lon"), P(None, "lat", "lon"), P(None, None, "lon")),
        check_vma=False,
    )
```
